32 devices in a mesh: dp: 2 (over x), ts: 16 (over z, y, core).
Axes of the slice: x: 2, y: 2, z: 4, core: 2. Of those that a mesh axis runs over, the one named last changes fastest.
Arguments:
- clip_video: bfloat16 [64, 4, 40, 128], P(('dp', 'ts')), may hold values from -6 to 6
- conv_weight: bfloat16 [3, 3, 3, 128, 128], replicated, may hold values from -0.109375 to 0.109375
- embed_weight: bfloat16 [128, 5120], replicated, may hold values from -0.5 to 0.5
- gain_spatial: float32 [5120], replicated, may hold values from 0.5 to 1.5
- gain_temporal: float32 [5120], replicated, may hold values from 0.5 to 1.5
- input_spatial: bfloat16 [5120, 384], P(('dp', 'ts')), may hold values from -0.078125 to 0.078125
- input_temporal: bfloat16 [5120, 384], P(('dp', 'ts')), may hold values from -0.078125 to 0.078125
- output_spatial: bfloat16 [128, 5120], replicated, may hold values from -2 to 2
- output_temporal: bfloat16 [128, 5120], replicated, may hold values from -2 to 2
- cotangent: bfloat16 [64, 4, 40, 5120], P(('dp', 'ts')), may hold values from -6 to 6
Outputs:
- layer_output: bfloat16 [64, 4, 40, 5120], P(('dp', 'ts'))
- grad_spatial: float32 [5120, 384], P(('dp', 'ts'))
The draws below stay inside these ranges and needn't reach their ends.
All inputs are finite; a program needn't handle non-finite values.
Results may differ from the reference program's by a relative error of at most 0.015.
Values may be sent and summed in bfloat16 or wider, within the bound.
A program may use at most 128 MiB of HBM per device.

```python
import jax
import jax.numpy as jnp
from jax import lax

D = 5120
HEAD = 128
CH = 128
FR = 16
H = 4
WC = 40
FRAMES = 64
N_DP = 2


def level_of(stream_key, extent, shards, least, largest):
    def one(position, blocks):
        heights = jax.random.uniform(jax.random.fold_in(jax.random.fold_in(stream_key, 6), position), (blocks,), jnp.float32, least / len(shards), largest / len(shards))
        return jnp.repeat(jnp.exp(heights), extent[position] // blocks).reshape((-1,) + (1,) * (len(extent) - position - 1))

    level = one(*shards[0])
    for cut in shards[1:]:
        level = level * one(*cut)
    return level


def bell_draw(stream_key, extent, scale, limit, split=(), dtype=jnp.bfloat16):
    factor_of = level_of(stream_key, extent, split, -0.22, 0.18) if split else 1.0
    drawn = jax.random.normal(stream_key, extent, jnp.float32) * scale * factor_of
    return jnp.minimum(jnp.maximum(drawn, -limit), limit).astype(dtype)


def setup_inputs(seed: int = 0) -> dict:
    keys = jax.random.split(jax.random.key(seed), 11)
    clip_video = bell_draw(keys[0], (FRAMES, H, WC, CH), 1.0, 6.0, ((0, 32),))
    conv_weight = bell_draw(keys[1], (3, 3, 3, CH, CH), (27 * CH) ** -0.5, 0.109375)
    embed_weight = bell_draw(keys[2], (CH, D), CH ** -0.5, 0.5)
    gain_spatial = jnp.clip(1.0 + 0.1 * jax.random.normal(keys[3], (D,), jnp.float32), 0.5, 1.5)
    gain_temporal = jnp.clip(1.0 + 0.1 * jax.random.normal(keys[4], (D,), jnp.float32), 0.5, 1.5)
    input_spatial = bell_draw(keys[5], (D, 3 * HEAD), D ** -0.5, 0.078125, ((0, 32),))
    input_temporal = bell_draw(keys[6], (D, 3 * HEAD), D ** -0.5, 0.078125, ((0, 32),))
    output_spatial = bell_draw(keys[7], (HEAD, D), (HEAD // 16) ** -0.5, 2.0)
    output_temporal = bell_draw(keys[8], (HEAD, D), (HEAD // 16) ** -0.5, 2.0)
    cotangent = bell_draw(keys[9], (FRAMES, H, WC, D), 1.0, 6.0, ((0, 32),))
    return {"clip_video": clip_video, "conv_weight": conv_weight, "embed_weight": embed_weight, "gain_spatial": gain_spatial, "gain_temporal": gain_temporal, "input_spatial": input_spatial, "input_temporal": input_temporal, "output_spatial": output_spatial, "output_temporal": output_temporal, "cotangent": cotangent}


epsilon = 1e-06
masked = -1e+30

def widen(array):
    return lax.optimization_barrier(array).astype(jnp.float32)

def conv_clips(video, weight):
    frames, height, columns, channels = video.shape
    out_channels = weight.shape[-1]
    volume = jnp.pad(video, ((2, 0), (1, 1), (1, 1), (0, 0)))
    summed = jnp.zeros((frames * height * columns, out_channels), jnp.float32)
    for time_tap in range(3):
        for row_tap in range(3):
            for col_tap in range(3):
                window = volume[2 - time_tap:2 - time_tap + frames, row_tap:row_tap + height, col_tap:col_tap + columns, :]
                summed = summed + jnp.dot(window.reshape(-1, channels), weight[time_tap, row_tap, col_tap], preferred_element_type=jnp.float32)
    return summed.reshape(frames, height, columns, out_channels)

def rms_norm(hidden, norm_gain):
    widened = hidden.astype(jnp.float32)
    factor = lax.rsqrt(lax.optimization_barrier(jnp.mean(widened * widened, axis=-1, keepdims=True)) + epsilon)
    return ((widened * factor * norm_gain).astype(jnp.bfloat16), factor)

def rms_norm_grad(hidden, norm_gain, factor, upstream):
    widened = hidden.astype(jnp.float32)
    scaled = upstream * norm_gain
    inner_mean = lax.optimization_barrier(jnp.mean(widened * scaled, axis=-1, keepdims=True))
    return factor * scaled - widened * factor ** 3 * inner_mean

def frame_forward(packed):
    frames, places, triple = packed.shape
    head_size = triple // 3
    flattened = widen(packed)
    queries = flattened[..., :head_size]
    key_rows = flattened[..., head_size:2 * head_size]
    values = flattened[..., 2 * head_size:]
    scores = jnp.einsum('fqd,fkd->fqk', queries, key_rows) * head_size ** (-0.5)
    attend = jax.nn.softmax(scores, axis=-1)
    rounded = widen(attend.astype(jnp.bfloat16))
    mixture = jnp.einsum('fqk,fkd->fqd', rounded, values)
    return (mixture.astype(jnp.bfloat16), attend)

def frame_backward(packed, attend, upstream):
    frames, places, triple = packed.shape
    head_size = triple // 3
    scale_factor = head_size ** (-0.5)
    flattened = widen(packed)
    queries = flattened[..., :head_size]
    key_rows = flattened[..., head_size:2 * head_size]
    values = flattened[..., 2 * head_size:]
    grad_out = widen(upstream)
    rounded = widen(attend.astype(jnp.bfloat16))
    grad_attend = jnp.einsum('fqd,fkd->fqk', grad_out, values)
    grad_values = jnp.einsum('fqk,fqd->fkd', rounded, grad_out)
    grad_scores = attend * (grad_attend - lax.optimization_barrier(jnp.sum(grad_attend * attend, axis=-1, keepdims=True)))
    grad_rounded = widen(grad_scores.astype(jnp.bfloat16))
    grad_queries = jnp.einsum('fqk,fkd->fqd', grad_rounded, key_rows) * scale_factor
    grad_keys = jnp.einsum('fqk,fqd->fkd', grad_rounded, queries) * scale_factor
    joined = jnp.concatenate([grad_queries, grad_keys, grad_values], axis=-1)
    return joined.astype(jnp.bfloat16)

def clip_forward(packed):
    frames, places, triple = packed.shape
    head_size = triple // 3
    volume = widen(packed.reshape(frames // FR, FR, places, triple))
    queries = volume[..., :head_size]
    key_rows = volume[..., head_size:2 * head_size]
    values = volume[..., 2 * head_size:]
    scores = jnp.einsum('cqpd,ckpd->cpqk', queries, key_rows) * head_size ** (-0.5)
    allowed = jnp.arange(FR)[:, None] >= jnp.arange(FR)[None, :]
    scores = jnp.where(allowed, scores, masked)
    attend = jax.nn.softmax(scores, axis=-1)
    rounded = widen(attend.astype(jnp.bfloat16))
    mixture = jnp.einsum('cpqk,ckpd->cqpd', rounded, values)
    return (mixture.astype(jnp.bfloat16).reshape(frames, places, head_size), attend)

def clip_backward(packed, attend, upstream):
    frames, places, triple = packed.shape
    head_size = triple // 3
    scale_factor = head_size ** (-0.5)
    volume = widen(packed.reshape(frames // FR, FR, places, triple))
    queries = volume[..., :head_size]
    key_rows = volume[..., head_size:2 * head_size]
    values = volume[..., 2 * head_size:]
    grad_out = widen(upstream.reshape(frames // FR, FR, places, head_size))
    rounded = widen(attend.astype(jnp.bfloat16))
    grad_attend = jnp.einsum('cqpd,ckpd->cpqk', grad_out, values)
    grad_values = jnp.einsum('cpqk,cqpd->ckpd', rounded, grad_out)
    grad_scores = attend * (grad_attend - lax.optimization_barrier(jnp.sum(grad_attend * attend, axis=-1, keepdims=True)))
    grad_rounded = widen(grad_scores.astype(jnp.bfloat16))
    grad_queries = jnp.einsum('cpqk,ckpd->cqpd', grad_rounded, key_rows) * scale_factor
    grad_keys = jnp.einsum('cpqk,cqpd->ckpd', grad_rounded, queries) * scale_factor
    joined = jnp.concatenate([grad_queries, grad_keys, grad_values], axis=-1)
    return joined.astype(jnp.bfloat16).reshape(frames, places, triple)

def reference(clip_video, conv_weight, embed_weight, gain_spatial, gain_temporal, input_spatial, input_temporal, output_spatial, output_temporal, cotangent):

    def group_pass(grad_first, inputs):
        group_video, group_cotangent = inputs
        features = jax.nn.gelu(conv_clips(group_video, conv_weight), approximate=True).astype(jnp.bfloat16)
        frames, height, columns, channels = features.shape
        places = height * columns
        tokens = frames * places
        embedded = jnp.dot(features.reshape(tokens, channels), embed_weight, preferred_element_type=jnp.float32).astype(jnp.bfloat16)
        normed_one, factor_one = rms_norm(embedded, gain_spatial)
        packed_one = jnp.dot(normed_one, input_spatial, preferred_element_type=jnp.float32).astype(jnp.bfloat16)
        packed_one = packed_one.reshape(frames, places, -1)
        mixture_one, attend_one = frame_forward(packed_one)
        after_space = (embedded.astype(jnp.float32) + jnp.dot(mixture_one.reshape(tokens, -1), output_spatial, preferred_element_type=jnp.float32)).astype(jnp.bfloat16)
        normed_two, factor_two = rms_norm(after_space, gain_temporal)
        packed_two = jnp.dot(normed_two, input_temporal, preferred_element_type=jnp.float32).astype(jnp.bfloat16)
        packed_two = packed_two.reshape(frames, places, -1)
        mixture_two, attend_two = clip_forward(packed_two)
        after_time = (after_space.astype(jnp.float32) + jnp.dot(mixture_two.reshape(tokens, -1), output_temporal, preferred_element_type=jnp.float32)).astype(jnp.bfloat16)
        cotangent_rows = group_cotangent.reshape(tokens, -1)
        grad_mix_two = jnp.dot(cotangent_rows, output_temporal.T, preferred_element_type=jnp.float32).astype(jnp.bfloat16)
        grad_packed_two = clip_backward(packed_two, attend_two, grad_mix_two.reshape(frames, places, -1)).reshape(tokens, -1)
        grad_normed_two = jnp.dot(grad_packed_two, input_temporal.T, preferred_element_type=jnp.float32)
        grad_after = (cotangent_rows.astype(jnp.float32) + rms_norm_grad(after_space, gain_temporal, factor_two, grad_normed_two)).astype(jnp.bfloat16)
        grad_mix_one = jnp.dot(grad_after, output_spatial.T, preferred_element_type=jnp.float32).astype(jnp.bfloat16)
        grad_packed_one = frame_backward(packed_one, attend_one, grad_mix_one.reshape(frames, places, -1)).reshape(tokens, -1)
        grad_first = grad_first + lax.dot_general(normed_one, grad_packed_one, (((0,), (0,)), ((), ())), preferred_element_type=jnp.float32)
        return (grad_first, after_time.reshape(frames, height, columns, -1))
    group_frames = clip_video.shape[0] // N_DP
    stacked_video = clip_video.reshape((N_DP, group_frames) + clip_video.shape[1:])
    stacked_cotangent = cotangent.reshape((N_DP, group_frames) + cotangent.shape[1:])
    zeros_grad = jnp.zeros(input_spatial.shape, jnp.float32)
    total, outputs = lax.scan(group_pass, zeros_grad, (stacked_video, stacked_cotangent))
    return (outputs.reshape(cotangent.shape), total)
```

```python
import jax
import jax.numpy as jnp
from jax import lax
from jax.sharding import PartitionSpec as P

FR = 16
epsilon = 1e-06
masked = -1e30
F32 = jnp.float32
BF16 = jnp.bfloat16


def mm(a, b, dims=((1,), (0,))):
    return lax.dot_general(a, b, (dims, ((), ())), preferred_element_type=F32)


def mm_t(a, b):
    return mm(a, b, ((1,), (1,)))


def t_mm(a, b):
    return mm(a, b, ((0,), (0,)))


def wide_mm(a, b):
    high = b.astype(BF16)
    low = (b - high.astype(F32)).astype(BF16)
    return mm(a, high) + mm(a, low)


def conv_local(volume, weight, count):
    frames, height, columns, channels = volume.shape
    padded = jnp.pad(volume, ((0, 0), (1, 1), (1, 1), (0, 0)))
    summed = jnp.zeros((count * height * columns, weight.shape[-1]), F32)
    for a in range(3):
        for b in range(3):
            for e in range(3):
                window = padded[2 - a : 2 - a + count, b : b + height, e : e + columns, :]
                summed = summed + mm(window.reshape(-1, channels), weight[a, b, e])
    return summed


def attend_forward(q, k, v, allowed):
    scores = mm_t(q, k) * q.shape[-1] ** -0.5
    scores = jnp.where(allowed, scores, masked)
    raised = jnp.exp(scores - jnp.max(scores, axis=-1, keepdims=True))
    attend = raised / jnp.sum(raised, axis=-1, keepdims=True)
    return mm(attend.astype(BF16), v).astype(BF16), attend


def attend_backward(q, k, v, attend, g):
    scale = q.shape[-1] ** -0.5
    grad_attend = mm_t(g, v)
    grad_values = t_mm(attend.astype(BF16), g)
    inner = jnp.sum(grad_attend * attend, axis=-1, keepdims=True)
    grad_scores = (attend * (grad_attend - inner)).astype(BF16)
    grad_q = mm(grad_scores, k) * scale
    grad_k = t_mm(grad_scores, q) * scale
    return jnp.concatenate([grad_q, grad_k, grad_values], axis=-1).astype(BF16)


def shards(
    clip_video,
    conv_weight,
    embed_weight,
    gain_spatial,
    gain_temporal,
    input_spatial,
    input_temporal,
    output_spatial,
    output_temporal,
    cotangent,
):
    frames, height, columns, channels = clip_video.shape
    rows, triple = input_spatial.shape
    head = triple // 3
    width = embed_weight.shape[-1]
    places = height * columns
    tokens = frames * places
    ts = lax.axis_size("ts")
    team = FR // frames
    share = places // team
    groups = [[c * team + i for i in range(team)] for c in range(ts // team)]
    me = lax.axis_index("dp") * ts + lax.axis_index("ts")

    route = [(i - 1, i) for i in range(1, ts)]
    prior = lax.ppermute(clip_video, "ts", route)
    volume = jnp.concatenate([prior, clip_video], axis=0)

    basis = jnp.concatenate([embed_weight, output_spatial], axis=0)
    window = lax.dynamic_slice(basis, (0, me * rows), (basis.shape[0], rows)).astype(F32)
    gain_s = lax.dynamic_slice(gain_spatial, (me * rows,), (rows,))
    gain_t = lax.dynamic_slice(gain_temporal, (me * rows,), (rows,))
    embed_rows = (window[:channels] * gain_s).astype(BF16)
    part = jnp.concatenate(
        [
            mm(embed_rows, input_spatial),
            mm((window * gain_t).astype(BF16), input_temporal),
        ],
        axis=0,
    )
    mixed = lax.psum(part.astype(BF16), ("dp", "ts"))
    map_space, map_time = mixed[:channels], mixed[channels:]
    gram = mm_t(basis, basis)
    cotangent_rows = cotangent.reshape(tokens, width)
    grad_mix_time = mm_t(cotangent_rows, output_temporal).astype(BF16)
    grad_direct = mm_t(cotangent_rows, output_spatial)

    features = jax.nn.gelu(conv_local(volume, conv_weight, frames), approximate=True).astype(BF16)
    squares = jnp.sum(
        wide_mm(features, gram[:channels, :channels]) * features.astype(F32), axis=-1, keepdims=True
    )
    factor_one = lax.rsqrt(jnp.maximum(squares, 0.0) / width + epsilon)
    packed_one = (mm(features, map_space) * factor_one).astype(BF16)
    place = jnp.arange(tokens)
    same_frame = (place[:, None] // places) == (place[None, :] // places)
    q, k, v = packed_one[:, :head], packed_one[:, head : 2 * head], packed_one[:, 2 * head :]
    mixture_one, attend_one = attend_forward(q, k, v, same_frame)
    joint = jnp.concatenate([features, mixture_one], axis=-1)
    spread = wide_mm(joint, gram)
    squares = jnp.sum(spread * joint.astype(F32), axis=-1, keepdims=True)
    factor_two = lax.rsqrt(jnp.maximum(squares, 0.0) / width + epsilon)
    packed_two = (mm(joint, map_time) * factor_two).astype(BF16)

    sent = jnp.concatenate([packed_two, grad_mix_time], axis=-1).reshape(frames, places, 4 * head)
    got = lax.all_to_all(
        sent, "ts", split_axis=1, concat_axis=0, tiled=True, axis_index_groups=groups
    ).reshape(FR * share, 4 * head)
    spot = jnp.arange(FR * share)
    allowed = ((spot[:, None] % share) == (spot[None, :] % share)) & (
        spot[:, None] >= spot[None, :]
    )
    tq, tk, tv, tg = (got[:, i * head : (i + 1) * head] for i in range(4))
    mixture_two, attend_two = attend_forward(tq, tk, tv, allowed)
    grad_two = attend_backward(tq, tk, tv, attend_two, tg)
    back = jnp.concatenate([mixture_two, grad_two], axis=-1).reshape(FR, share, 4 * head)
    home = lax.all_to_all(
        back, "ts", split_axis=0, concat_axis=1, tiled=True, axis_index_groups=groups
    ).reshape(tokens, 4 * head)
    mixture_two, grad_two = home[:, :head], home[:, head:]

    output = mm(
        jnp.concatenate([joint, mixture_two], axis=-1),
        jnp.concatenate([basis, output_temporal], axis=0),
    ).astype(BF16)

    inner = jnp.sum(grad_two.astype(F32) * packed_two.astype(F32), axis=-1, keepdims=True)
    grad_mix_one = (
        grad_direct
        + factor_two * mm_t(grad_two, map_time[channels:])
        - (factor_two**2 * inner / width) * spread[:, channels:]
    ).astype(BF16)
    grad_one = attend_backward(q, k, v, attend_one, grad_mix_one)
    scaled = (features.astype(F32) * factor_one).astype(BF16)
    core = lax.psum(t_mm(scaled, grad_one).astype(BF16), ("dp", "ts"))
    return output.reshape(frames, height, columns, width), t_mm(embed_rows, core)


def solution(mesh):
    placed = (
        P(("dp", "ts"), None, None, None),
        P(),
        P(),
        P(),
        P(),
        P(("dp", "ts"), None),
        P(("dp", "ts"), None),
        P(),
        P(),
        P(("dp", "ts"), None, None, None),
    )
    return jax.shard_map(
        shards,
        mesh=mesh,
        in_specs=placed,
        out_specs=(P(("dp", "ts"), None, None, None), P(("dp", "ts"), None)),
        check_vma=False,
    )
```

```python
import functools

import jax
import jax.numpy as jnp
import numpy as np
from jax import lax
from jax.experimental import pallas as pl
from jax.experimental.pallas import tpu as pltpu
from jax.sharding import PartitionSpec as P

FR = 16
REDUCERS = 24
epsilon = 1e-06
masked = -1e30
F32 = jnp.float32
BF16 = jnp.bfloat16
MESH = pl.DeviceIdType.MESH


def mm(a, b, dims=((1,), (0,))):
    return lax.dot_general(a, b, (dims, ((), ())), preferred_element_type=F32)


def mm_t(a, b):
    return mm(a, b, ((1,), (1,)))


def t_mm(a, b):
    return mm(a, b, ((0,), (0,)))


def wide_mm(a, b):
    high = b.astype(BF16)
    low = (b - high.astype(F32)).astype(BF16)
    return mm(a, high) + mm(a, low)


def attend_forward(q, k, v, bias):
    scores = mm_t(q, k) * q.shape[-1] ** -0.5 + bias.astype(F32)
    raised = jnp.exp(scores - jnp.max(scores, axis=-1, keepdims=True))
    attend = raised / jnp.sum(raised, axis=-1, keepdims=True)
    return mm(attend.astype(BF16), v).astype(BF16), attend


def attend_backward(q, k, v, attend, g):
    scale = q.shape[-1] ** -0.5
    grad_attend = mm_t(g, v)
    grad_values = t_mm(attend.astype(BF16), g)
    inner = jnp.sum(grad_attend * attend, axis=-1, keepdims=True)
    grad_scores = (attend * (grad_attend - inner)).astype(BF16)
    grad_q = mm(grad_scores, k) * scale
    grad_k = t_mm(grad_scores, q) * scale
    return jnp.concatenate([grad_q, grad_k, grad_values], axis=-1).astype(BF16)


def stacked(block):
    third = block.shape[1] // 3
    return jnp.concatenate([block[:, i * third : (i + 1) * third] for i in range(3)], axis=0)


def unstacked(block):
    third = block.shape[0] // 3
    return jnp.concatenate([block[i * third : (i + 1) * third] for i in range(3)], axis=1)


def moved(block, distance):
    if distance == 0:
        return block
    return pltpu.roll(block, distance % block.shape[0], 0)


def whole_kernel(
    dims,
    video_hbm, conv_hbm, embed_hbm, gain_s_hbm, gain_t_hbm, in_s_hbm, in_t_hbm, out_s_hbm,
    out_t_hbm, cot_hbm, perm_hbm, frame_bias_hbm, clip_bias_hbm, edge_hbm,
    result, grad_result,
    video, prior, taps, basis, gain_s, gain_t, in_s, in_t, cot, perm, frame_bias, clip_bias, edge,
    part_a, part_b, part_c, land_a, land_b, land_c, full_a, full_b, full_c,
    sent, got, back, home, gram, direct,
    local_sem, send_sem, recv_sem,
):
    n_dp, n_ts, frames, places, columns, team, share, pad, rows, window = dims
    n = n_dp * n_ts
    head = 128
    width = basis.shape[1]
    tokens = frames * places
    dp, ts = lax.axis_index("dp"), lax.axis_index("ts")
    me = dp * n_ts + ts

    loads = [
        (in_s_hbm, in_s), (in_t_hbm, in_t), (gain_s_hbm, gain_s), (gain_t_hbm, gain_t),
        (embed_hbm, basis.at[0:head]), (out_s_hbm, basis.at[head : 2 * head]),
        (video_hbm, video), (edge_hbm, edge), (conv_hbm, taps), (frame_bias_hbm, frame_bias),
        (perm_hbm, perm), (out_t_hbm, basis.at[2 * head : 3 * head]), (cot_hbm, cot),
        (clip_bias_hbm, clip_bias),
    ]
    copies = [pltpu.make_async_copy(s, d, local_sem.at[i]) for i, (s, d) in enumerate(loads)]
    for copy in copies:
        copy.start()

    barrier = pltpu.get_barrier_semaphore()

    def greet(i, carry):
        dev = lax.rem(me + i, n)
        pl.semaphore_signal(
            barrier, inc=1, device_id=(dev // n_ts, lax.rem(dev, n_ts)), device_id_type=MESH
        )
        return carry

    lax.fori_loop(1, n, greet, 0)

    def remote(src, dst, index, dev):
        return pltpu.make_async_remote_copy(
            src_ref=src, dst_ref=dst, send_sem=send_sem.at[index], recv_sem=recv_sem.at[index],
            device_id=(dev // n_ts, lax.rem(dev, n_ts)), device_id_type=MESH,
        )

    def settle(ref, count, sem):
        piece = ref.at[pl.ds(0, count)]
        pltpu.make_async_copy(piece, piece, sem).wait()

    reducing = lax.rem(me, 4) != 3
    inside = me < REDUCERS // 3 * 4
    leads = jnp.logical_and(reducing, inside)
    mine = (me // 4) * 3 + lax.rem(me, 4)

    def scatter(part, land, index):
        def step(i, carry):
            r = lax.rem(me + i, REDUCERS)
            dev = r + r // 3

            @pl.when(dev != me)
            def _():
                remote(part.at[r], land.at[me], index, dev).start()

            return carry

        lax.fori_loop(0, REDUCERS, step, 0)

    def gather(part, land, full, index):
        @pl.when(leads)
        def _():
            land[pl.ds(me, 1)] = part[pl.ds(mine, 1)]
            settle(land, n - 1, recv_sem.at[index])
            total = jnp.sum(land[...].astype(F32), axis=0, keepdims=True)
            full[pl.ds(mine, 1)] = total.astype(BF16)

            def step(i, carry):
                dev = lax.rem(me + i, n)
                remote(full.at[mine], full.at[mine], index + 1, dev).start()
                return carry

            lax.fori_loop(1, n, step, 0)

    def collect(part, land, full, index):
        @pl.when(leads)
        def _():
            settle(full, REDUCERS - 1, recv_sem.at[index + 1])
            settle(part, REDUCERS - 1, send_sem.at[index])
            settle(land, n - 1, send_sem.at[index + 1])

        @pl.when(jnp.logical_not(leads))
        def _():
            settle(full, REDUCERS, recv_sem.at[index + 1])
            settle(part, REDUCERS, send_sem.at[index])

        return unstacked(full[...].reshape(-1, head))

    for copy in copies[:6]:
        copy.wait()
    first = me * rows
    start = pl.multiple_of(first // 128 * 128, 128)
    if (n * rows - rows) // 128 * 128 + window > width:
        limit = width - window
        start = pl.multiple_of(jnp.where(start > limit, limit, start), 128)
    shift = first - start
    place = lax.broadcasted_iota(jnp.int32, (window, rows), 0)
    source = lax.broadcasted_iota(jnp.int32, (window, rows), 1)
    chosen = jnp.where(place == source + shift, 1.0, 0.0).astype(BF16)
    spread_s = mm(chosen, in_s[...]).astype(BF16)
    spread_t = mm(chosen, in_t[...]).astype(BF16)
    span = basis[0 : 2 * head, pl.ds(start, window)].astype(F32)
    span_s = (span[:head] * gain_s[:, pl.ds(start, window)]).astype(BF16)
    span_t = (span * gain_t[:, pl.ds(start, window)]).astype(BF16)
    part_a[...] = stacked(mm(span_s, spread_s)).astype(BF16).reshape(part_a.shape)
    part_b[...] = stacked(mm(span_t, spread_t)).astype(BF16).reshape(part_b.shape)
    copies[6].wait()

    pl.semaphore_wait(barrier, n - 1)
    halo = remote(video.at[pl.ds(frames - 2, 2)], prior, 0, me + 1)
    halo_in = remote(video.at[pl.ds(frames - 2, 2)], prior, 0, me)

    @pl.when(ts < n_ts - 1)
    def _():
        halo.start()

    scatter(part_a, land_a, 1)
    scatter(part_b, land_b, 3)
    embed_rows = mm(span_s, chosen).astype(BF16)

    @pl.when(ts == 0)
    def _():
        prior[...] = jnp.zeros_like(prior)

    @pl.when(ts > 0)
    def _():
        halo_in.wait_recv()

    for copy in copies[7:11]:
        copy.wait()
    volume = jnp.concatenate([prior[...], video[...]], axis=0)
    deep = jnp.concatenate(
        [volume[2 - a : 2 - a + frames].reshape(tokens, head) for a in range(3)], axis=1
    )
    edges = edge[...].astype(F32)
    by_col = [None, None, None]
    for b in range(3):
        weight = jnp.concatenate(
            [jnp.concatenate([taps[a, b, e] for a in range(3)], axis=0) for e in range(3)], axis=1
        )
        product = mm(deep, weight)
        product = moved(product, -(b - 1) * columns)
        if b == 0:
            product = product * edges[:, 0:1]
        if b == 2:
            product = product * edges[:, 1:2]
        for e in range(3):
            piece = product[:, e * head : (e + 1) * head]
            by_col[e] = piece if by_col[e] is None else by_col[e] + piece
    summed = (
        by_col[1] + moved(by_col[0], 1) * edges[:, 2:3] + moved(by_col[2], -1) * edges[:, 3:4]
    )
    features = jax.nn.gelu(summed, approximate=True).astype(BF16)

    gather(part_a, land_a, full_a, 1)

    for copy in copies[11:]:
        copy.wait()
    chunk = width // 5
    gram[...] = jnp.zeros_like(gram)
    direct[...] = jnp.zeros_like(direct)

    def slab(i, carry):
        cols = pl.ds(pl.multiple_of(i * chunk, 128), chunk)
        pair = basis[0 : 2 * head, cols]
        gram[...] += mm_t(pair, pair)
        direct[...] += mm_t(cot[:, cols], basis[head : 3 * head, cols])
        return carry

    lax.fori_loop(0, 5, slab, 0)
    grad_mix_time = direct[:, head:].astype(BF16)
    grams = gram[...]

    gather(part_b, land_b, full_b, 3)

    squares = jnp.sum(
        wide_mm(features, grams[:head, :head]) * features.astype(F32), axis=-1, keepdims=True
    )
    factor_one = lax.rsqrt(jnp.maximum(squares, 0.0) / width + epsilon)
    map_space = collect(part_a, land_a, full_a, 1)
    packed_one = (mm(features, map_space) * factor_one).astype(BF16)
    q, k, v = packed_one[:, :head], packed_one[:, head : 2 * head], packed_one[:, 2 * head :]
    mixture_one, attend_one = attend_forward(q, k, v, frame_bias[...])
    joint = jnp.concatenate([features, mixture_one], axis=-1)
    spread = wide_mm(joint, grams)
    squares = jnp.sum(spread * joint.astype(F32), axis=-1, keepdims=True)
    factor_two = lax.rsqrt(jnp.maximum(squares, 0.0) / width + epsilon)
    map_time = collect(part_b, land_b, full_b, 3)
    packed_two = (mm(joint, map_time) * factor_two).astype(BF16)

    seat = lax.rem(ts, team)
    base = me - seat
    order = perm[...]

    def swap(source_ref, target_ref, index):
        def step(i, carry):
            other = lax.rem(seat + i, team)
            remote(source_ref.at[other], target_ref.at[seat], index, base + other).start()
            return carry

        lax.fori_loop(1, team, step, 0)
        target_ref[pl.ds(seat, 1)] = source_ref[pl.ds(seat, 1)]

    sent[...] = (
        mm(order, jnp.concatenate([packed_two, grad_mix_time], axis=-1))
        .astype(BF16)
        .reshape(sent.shape)
    )
    swap(sent, got, 5)
    settle(got, team - 1, recv_sem.at[5])
    arrived = got[...].reshape(team * pad, 4 * head)
    tq, tk, tv, tg = (arrived[:, i * head : (i + 1) * head] for i in range(4))
    mixture_two, attend_two = attend_forward(tq, tk, tv, clip_bias[...])
    grad_two = attend_backward(tq, tk, tv, attend_two, tg)
    back[...] = jnp.concatenate([mixture_two, grad_two], axis=-1).reshape(back.shape)
    swap(back, home, 6)
    settle(home, team - 1, recv_sem.at[6])
    returned = t_mm(order, home[...].reshape(team * pad, 4 * head)).astype(BF16)
    mixture_two, grad_two = returned[:, :head], returned[:, head:]

    inner = jnp.sum(grad_two.astype(F32) * packed_two.astype(F32), axis=-1, keepdims=True)
    grad_mix_one = (
        direct[:, :head]
        + factor_two * mm_t(grad_two, map_time[head:])
        - (factor_two * factor_two * inner / width) * spread[:, head:]
    ).astype(BF16)
    grad_one = attend_backward(q, k, v, attend_one, grad_mix_one)
    scaled = (features.astype(F32) * factor_one).astype(BF16)
    part_c[...] = stacked(t_mm(scaled, grad_one)).astype(BF16).reshape(part_c.shape)
    scatter(part_c, land_c, 7)

    triple = jnp.concatenate([joint, mixture_two], axis=-1)

    def write(i, carry):
        cols = pl.ds(pl.multiple_of(i * chunk, 128), chunk)
        result[:, cols] = mm(triple, basis[:, cols]).astype(BF16)
        return carry

    lax.fori_loop(0, 2, write, 0)
    gather(part_c, land_c, full_c, 7)
    lax.fori_loop(2, 5, write, 0)
    total = collect(part_c, land_c, full_c, 7)
    grad_result[...] = t_mm(embed_rows, total)

    @pl.when(ts < n_ts - 1)
    def _():
        halo.wait_send()

    settle(sent, team - 1, send_sem.at[5])
    settle(back, team - 1, send_sem.at[6])


def shards(
    clip_video, conv_weight, embed_weight, gain_spatial, gain_temporal, input_spatial,
    input_temporal, output_spatial, output_temporal, cotangent,
):
    frames, height, columns, channels = clip_video.shape
    rows, triple = input_spatial.shape
    head = triple // 3
    width = embed_weight.shape[-1]
    places = height * columns
    tokens = frames * places
    n_dp, n_ts = lax.axis_size("dp"), lax.axis_size("ts")
    n = n_dp * n_ts
    team = FR // frames
    share = places // team
    pad = -(-frames * share // 16) * 16
    reach = max(i * rows % 128 + rows for i in range(n))
    window = -(-reach // 128) * 128

    token = np.arange(tokens)
    frame, spot = token // places, token % places
    slot = spot // share * pad + frame * share + spot % share
    perm = np.zeros((team * pad, tokens), np.float32)
    perm[slot, token] = 1.0
    frame_bias = np.where(frame[:, None] == frame[None, :], 0.0, masked)
    seat = np.arange(team * pad)
    local = seat % pad
    when = seat // pad * frames + local // share
    valid = local < frames * share
    allowed = (
        (local[:, None] % share == local[None, :] % share)
        & (when[:, None] >= when[None, :])
        & valid[:, None]
        & valid[None, :]
    )
    clip_bias = np.where(allowed, 0.0, masked)
    edge = np.zeros((tokens, 128), np.float32)
    edge[:, 0] = spot // columns >= 1
    edge[:, 1] = spot // columns < height - 1
    edge[:, 2] = spot % columns >= 1
    edge[:, 3] = spot % columns < columns - 1

    dims = (n_dp, n_ts, frames, places, columns, team, share, pad, rows, window)
    any_space = pl.BlockSpec(memory_space=pl.ANY)
    vmem = pl.BlockSpec(memory_space=pltpu.VMEM)
    buffer = lambda *shape: pltpu.VMEM(shape, BF16)
    wide = lambda *shape: pltpu.VMEM(shape, F32)
    output, grad = pl.pallas_call(
        functools.partial(whole_kernel, dims),
        out_shape=(
            jax.ShapeDtypeStruct((tokens, width), BF16),
            jax.ShapeDtypeStruct((rows, triple), F32),
        ),
        in_specs=[any_space] * 14,
        out_specs=(vmem, vmem),
        scratch_shapes=[
            buffer(frames, places, channels), buffer(2, places, channels),
            buffer(*conv_weight.shape), buffer(3 * head, width), wide(1, width), wide(1, width),
            buffer(rows, triple), buffer(rows, triple), buffer(tokens, width),
            buffer(team * pad, tokens), buffer(tokens, tokens), buffer(team * pad, team * pad),
            buffer(tokens, 128),
            buffer(REDUCERS, 16, 128), buffer(REDUCERS, 32, 128), buffer(REDUCERS, 16, 128),
            buffer(n, 16, 128), buffer(n, 32, 128), buffer(n, 16, 128),
            buffer(REDUCERS, 16, 128), buffer(REDUCERS, 32, 128), buffer(REDUCERS, 16, 128),
            buffer(team, pad, 4 * head), buffer(team, pad, 4 * head),
            buffer(team, pad, 4 * head), buffer(team, pad, 4 * head),
            wide(2 * head, 2 * head), wide(tokens, 2 * head),
            pltpu.SemaphoreType.DMA((14,)), pltpu.SemaphoreType.DMA((9,)),
            pltpu.SemaphoreType.DMA((9,)),
        ],
        compiler_params=pltpu.CompilerParams(
            collective_id=0, has_side_effects=True, vmem_limit_bytes=56 * 1024 * 1024
        ),
    )(
        clip_video.reshape(frames, places, channels),
        conv_weight,
        embed_weight,
        gain_spatial.reshape(1, width),
        gain_temporal.reshape(1, width),
        input_spatial,
        input_temporal,
        output_spatial,
        output_temporal,
        cotangent.reshape(tokens, width),
        jnp.asarray(perm, BF16),
        jnp.asarray(frame_bias, BF16),
        jnp.asarray(clip_bias, BF16),
        jnp.asarray(edge, BF16),
    )
    return output.reshape(frames, height, columns, width), grad


def solution(mesh):
    placed = (
        P(("dp", "ts"), None, None, None), P(), P(), P(), P(), P(("dp", "ts"), None),
        P(("dp", "ts"), None), P(), P(), P(("dp", "ts"), None, None, None),
    )
    return jax.shard_map(
        shards,
        mesh=mesh,
        in_specs=placed,
        out_specs=(P(("dp", "ts"), None, None, None), P(("dp", "ts"), None)),
        check_vma=False,
    )
```

```python
import functools

import jax
import jax.numpy as jnp
import numpy as np
from jax import lax
from jax.experimental import pallas as pl
from jax.experimental.pallas import tpu as pltpu
from jax.sharding import PartitionSpec as P

FR = 16
REDUCERS = 16
epsilon = 1e-06
masked = -1e30
F32 = jnp.float32
BF16 = jnp.bfloat16
MESH = pl.DeviceIdType.MESH


def mm(a, b, dims=((1,), (0,))):
    return lax.dot_general(a, b, (dims, ((), ())), preferred_element_type=F32)


def mm_t(a, b):
    return mm(a, b, ((1,), (1,)))


def t_mm(a, b):
    return mm(a, b, ((0,), (0,)))


def wide_mm(a, b):
    high = b.astype(BF16)
    low = (b - high.astype(F32)).astype(BF16)
    return mm(a, high) + mm(a, low)


def attend_forward(q, k, v, bias):
    scores = mm_t(q, k) * q.shape[-1] ** -0.5 + bias.astype(F32)
    raised = jnp.exp(scores - jnp.max(scores, axis=-1, keepdims=True))
    attend = raised / jnp.sum(raised, axis=-1, keepdims=True)
    return mm(attend.astype(BF16), v).astype(BF16), attend


def attend_backward(q, k, v, attend, g):
    scale = q.shape[-1] ** -0.5
    grad_attend = mm_t(g, v)
    grad_values = t_mm(attend.astype(BF16), g)
    inner = jnp.sum(grad_attend * attend, axis=-1, keepdims=True)
    grad_scores = (attend * (grad_attend - inner)).astype(BF16)
    grad_q = mm(grad_scores, k) * scale
    grad_k = t_mm(grad_scores, q) * scale
    return jnp.concatenate([grad_q, grad_k, grad_values], axis=-1).astype(BF16)


def stacked(block):
    third = block.shape[1] // 3
    return jnp.concatenate([block[:, i * third : (i + 1) * third] for i in range(3)], axis=0)


def unstacked(block):
    third = block.shape[0] // 3
    return jnp.concatenate([block[i * third : (i + 1) * third] for i in range(3)], axis=1)


def moved(block, distance):
    if distance == 0:
        return block
    return pltpu.roll(block, distance % block.shape[0], 0)


def whole_kernel(
    dims,
    video_hbm, conv_hbm, embed_hbm, gain_s_hbm, gain_t_hbm, in_s_hbm, in_t_hbm, out_s_hbm,
    out_t_hbm, cot_hbm, perm_hbm, frame_bias_hbm, clip_bias_hbm, edge_hbm,
    result, grad_result,
    video, prior, taps, basis, gain_s, gain_t, in_s, in_t, cot, perm, frame_bias, clip_bias, edge,
    part_a, part_b, part_c, land_a, land_b, land_c, full_a, full_b, full_c,
    sent, got, sent_g, got_g, back, home, back_m, home_m, gram, direct,
    local_sem, send_sem, recv_sem,
):
    n_dp, n_ts, frames, places, columns, team, share, pad, rows, window = dims
    n = n_dp * n_ts
    head = 128
    width = basis.shape[1]
    tokens = frames * places
    dp, ts = lax.axis_index("dp"), lax.axis_index("ts")
    me = dp * n_ts + ts

    loads = [
        (in_s_hbm, in_s), (in_t_hbm, in_t), (gain_s_hbm, gain_s), (gain_t_hbm, gain_t),
        (embed_hbm, basis.at[0:head]), (out_s_hbm, basis.at[head : 2 * head]),
        (video_hbm, video), (edge_hbm, edge), (conv_hbm, taps), (frame_bias_hbm, frame_bias),
        (perm_hbm, perm), (out_t_hbm, basis.at[2 * head : 3 * head]), (cot_hbm, cot),
        (clip_bias_hbm, clip_bias),
    ]
    copies = [pltpu.make_async_copy(s, d, local_sem.at[i]) for i, (s, d) in enumerate(loads)]
    for copy in copies:
        copy.start()

    barrier = pltpu.get_barrier_semaphore()

    def greet(i, carry):
        dev = lax.rem(me + i, n)
        pl.semaphore_signal(
            barrier, inc=1, device_id=(dev // n_ts, lax.rem(dev, n_ts)), device_id_type=MESH
        )
        return carry

    lax.fori_loop(1, n, greet, 0)

    def remote(src, dst, index, dev):
        return pltpu.make_async_remote_copy(
            src_ref=src, dst_ref=dst, send_sem=send_sem.at[index], recv_sem=recv_sem.at[index],
            device_id=(dev // n_ts, lax.rem(dev, n_ts)), device_id_type=MESH,
        )

    def settle(ref, count, sem):
        piece = ref.at[pl.ds(0, count)]
        pltpu.make_async_copy(piece, piece, sem).wait()

    half, quarter = n_ts // 2, n_ts // 4
    mine = dp * half + ts - quarter
    leads = jnp.logical_and(
        jnp.logical_and(ts >= quarter, ts < quarter + half), mine < REDUCERS
    )

    def scatter(part, land, index):
        def step(i, carry):
            r = lax.rem(me + i, REDUCERS)
            dev = r // half * n_ts + quarter + lax.rem(r, half)

            @pl.when(dev != me)
            def _():
                remote(part.at[r], land.at[me], index, dev).start()

            return carry

        lax.fori_loop(0, REDUCERS, step, 0)

    def gather(part, land, full, index):
        @pl.when(leads)
        def _():
            land[pl.ds(me, 1)] = part[pl.ds(mine, 1)]
            settle(land, n - 1, recv_sem.at[index])
            total = jnp.sum(land[...].astype(F32), axis=0, keepdims=True)
            full[pl.ds(mine, 1)] = total.astype(BF16)

            def step(i, carry):
                dev = lax.rem(me + i, n)
                remote(full.at[mine], full.at[mine], index + 1, dev).start()
                return carry

            lax.fori_loop(1, n, step, 0)

    def collect(part, land, full, index):
        @pl.when(leads)
        def _():
            settle(full, REDUCERS - 1, recv_sem.at[index + 1])
            settle(part, REDUCERS - 1, send_sem.at[index])
            settle(land, n - 1, send_sem.at[index + 1])

        @pl.when(jnp.logical_not(leads))
        def _():
            settle(full, REDUCERS, recv_sem.at[index + 1])
            settle(part, REDUCERS, send_sem.at[index])

        return unstacked(full[...].astype(F32).reshape(-1, head)).astype(BF16)

    for copy in copies[:6]:
        copy.wait()
    first = me * rows
    start = pl.multiple_of(first // 128 * 128, 128)
    if (n * rows - rows) // 128 * 128 + window > width:
        limit = width - window
        start = pl.multiple_of(jnp.where(start > limit, limit, start), 128)
    shift = first - start
    place = lax.broadcasted_iota(jnp.int32, (window, rows), 0)
    source = lax.broadcasted_iota(jnp.int32, (window, rows), 1)
    chosen = jnp.where(place == source + shift, 1.0, 0.0).astype(BF16)
    spread_s = mm(chosen, in_s[...]).astype(BF16)
    spread_t = mm(chosen, in_t[...]).astype(BF16)
    span = basis[0 : 2 * head, pl.ds(start, window)].astype(F32)
    span_s = (span[:head] * gain_s[:, pl.ds(start, window)]).astype(BF16)
    span_t = (span * gain_t[:, pl.ds(start, window)]).astype(BF16)
    part_a[...] = stacked(mm(span_s, spread_s)).reshape(part_a.shape).astype(BF16)
    part_b[...] = stacked(mm(span_t, spread_t)).reshape(part_b.shape).astype(BF16)
    copies[6].wait()

    pl.semaphore_wait(barrier, n - 1)
    halo = remote(video.at[pl.ds(frames - 2, 2)], prior, 0, me + 1)
    halo_in = remote(video.at[pl.ds(frames - 2, 2)], prior, 0, me)

    @pl.when(ts < n_ts - 1)
    def _():
        halo.start()

    scatter(part_a, land_a, 1)
    scatter(part_b, land_b, 3)
    embed_rows = mm(span_s, chosen).astype(BF16)

    @pl.when(ts == 0)
    def _():
        prior[...] = jnp.zeros_like(prior)

    @pl.when(ts > 0)
    def _():
        halo_in.wait_recv()

    for copy in copies[7:11]:
        copy.wait()
    volume = jnp.concatenate([prior[...], video[...]], axis=0)
    deep = jnp.concatenate(
        [volume[2 - a : 2 - a + frames].reshape(tokens, head) for a in range(3)], axis=1
    )
    edges = edge[...].astype(F32)
    by_col = [None, None, None]
    for b in range(3):
        weight = jnp.concatenate(
            [jnp.concatenate([taps[a, b, e] for a in range(3)], axis=0) for e in range(3)], axis=1
        )
        product = mm(deep, weight)
        product = moved(product, -(b - 1) * columns)
        if b == 0:
            product = product * edges[:, 0:1]
        if b == 2:
            product = product * edges[:, 1:2]
        for e in range(3):
            piece = product[:, e * head : (e + 1) * head]
            by_col[e] = piece if by_col[e] is None else by_col[e] + piece
    summed = (
        by_col[1] + moved(by_col[0], 1) * edges[:, 2:3] + moved(by_col[2], -1) * edges[:, 3:4]
    )
    features = jax.nn.gelu(summed, approximate=True).astype(BF16)

    gather(part_a, land_a, full_a, 1)

    for copy in copies[11:]:
        copy.wait()
    chunk = width // 5
    gram[...] = jnp.zeros_like(gram)
    direct[...] = jnp.zeros_like(direct)

    def slab(i, carry):
        cols = pl.ds(pl.multiple_of(i * chunk, 128), chunk)
        pair = basis[0 : 2 * head, cols]
        gram[...] += mm_t(pair, pair)
        direct[...] += mm_t(cot[:, cols], basis[head : 3 * head, cols])
        return carry

    lax.fori_loop(0, 5, slab, 0)
    grad_mix_time = direct[:, head:].astype(BF16)
    grams = gram[...]

    seat = lax.rem(ts, team)
    base = me - seat
    order = perm[...]

    def swap(source_ref, target_ref, index):
        def step(i, carry):
            other = lax.rem(seat + i, team)
            remote(source_ref.at[other], target_ref.at[seat], index, base + other).start()
            return carry

        lax.fori_loop(1, team, step, 0)
        target_ref[pl.ds(seat, 1)] = source_ref[pl.ds(seat, 1)]

    def dealt(values, ref):
        ref[...] = mm(order, values).reshape(ref.shape).astype(BF16)

    def received(ref, index):
        settle(ref, team - 1, recv_sem.at[index])
        return ref[...].astype(F32).reshape(team * pad, -1).astype(BF16)

    dealt(grad_mix_time, sent_g)
    swap(sent_g, got_g, 9)
    gather(part_b, land_b, full_b, 3)

    squares = jnp.sum(
        wide_mm(features, grams[:head, :head]) * features.astype(F32), axis=-1, keepdims=True
    )
    factor_one = lax.rsqrt(jnp.maximum(squares, 0.0) / width + epsilon)
    map_space = collect(part_a, land_a, full_a, 1)
    packed_one = (mm(features, map_space) * factor_one).astype(BF16)
    q, k, v = packed_one[:, :head], packed_one[:, head : 2 * head], packed_one[:, 2 * head :]
    mixture_one, attend_one = attend_forward(q, k, v, frame_bias[...])
    joint = jnp.concatenate([features, mixture_one], axis=-1)
    spread = wide_mm(joint, grams)
    squares = jnp.sum(spread * joint.astype(F32), axis=-1, keepdims=True)
    factor_two = lax.rsqrt(jnp.maximum(squares, 0.0) / width + epsilon)
    map_time = collect(part_b, land_b, full_b, 3)
    packed_two = (mm(joint, map_time) * factor_two).astype(BF16)

    dealt(packed_two, sent)
    swap(sent, got, 5)
    tg = received(got_g, 9)
    arrived = received(got, 5)
    tq, tk, tv = (arrived[:, i * head : (i + 1) * head] for i in range(3))
    mixture_two, attend_two = attend_forward(tq, tk, tv, clip_bias[...])
    grad_two = attend_backward(tq, tk, tv, attend_two, tg)
    back[...] = grad_two.astype(F32).reshape(back.shape).astype(BF16)
    swap(back, home, 6)
    back_m[...] = mixture_two.astype(F32).reshape(back_m.shape).astype(BF16)
    swap(back_m, home_m, 10)
    grad_two = t_mm(order, received(home, 6)).astype(BF16)

    inner = jnp.sum(grad_two.astype(F32) * packed_two.astype(F32), axis=-1, keepdims=True)
    grad_mix_one = (
        direct[:, :head]
        + factor_two * mm_t(grad_two, map_time[head:])
        - (factor_two * factor_two * inner / width) * spread[:, head:]
    ).astype(BF16)
    grad_one = attend_backward(q, k, v, attend_one, grad_mix_one)
    scaled = (features.astype(F32) * factor_one).astype(BF16)
    part_c[...] = stacked(t_mm(scaled, grad_one)).reshape(part_c.shape).astype(BF16)
    scatter(part_c, land_c, 7)

    mixture_two = t_mm(order, received(home_m, 10)).astype(BF16)
    result[...] = jnp.concatenate([joint, mixture_two], axis=-1)
    gather(part_c, land_c, full_c, 7)
    total = collect(part_c, land_c, full_c, 7)
    grad_result[...] = t_mm(embed_rows, total)

    @pl.when(ts < n_ts - 1)
    def _():
        halo.wait_send()

    settle(sent, team - 1, send_sem.at[5])
    settle(back, team - 1, send_sem.at[6])
    settle(sent_g, team - 1, send_sem.at[9])
    settle(back_m, team - 1, send_sem.at[10])


def final_kernel(factors, grad, embed, out_s, out_t, output, grad_result):
    weight = jnp.concatenate([embed[...], out_s[...], out_t[...]], axis=0)
    output[...] = mm(factors[...], weight).astype(BF16)

    @pl.when(pl.program_id(0) == 0)
    def _():
        grad_result[...] = grad[...]


def shards(
    clip_video, conv_weight, embed_weight, gain_spatial, gain_temporal, input_spatial,
    input_temporal, output_spatial, output_temporal, cotangent,
):
    frames, height, columns, channels = clip_video.shape
    rows, triple = input_spatial.shape
    head = triple // 3
    width = embed_weight.shape[-1]
    places = height * columns
    tokens = frames * places
    n_dp, n_ts = lax.axis_size("dp"), lax.axis_size("ts")
    n = n_dp * n_ts
    team = FR // frames
    share = places // team
    pad = -(-frames * share // 8) * 8
    reach = max(i * rows % 128 + rows for i in range(n))
    window = -(-reach // 128) * 128

    token = np.arange(tokens)
    frame, spot = token // places, token % places
    slot = spot // share * pad + frame * share + spot % share
    perm = np.zeros((team * pad, tokens), np.float32)
    perm[slot, token] = 1.0
    frame_bias = np.where(frame[:, None] == frame[None, :], 0.0, masked)
    seat = np.arange(team * pad)
    local = seat % pad
    when = seat // pad * frames + local // share
    valid = local < frames * share
    allowed = (
        (local[:, None] % share == local[None, :] % share)
        & (when[:, None] >= when[None, :])
        & valid[:, None]
        & valid[None, :]
    )
    clip_bias = np.where(allowed, 0.0, masked)
    edge = np.zeros((tokens, 128), np.float32)
    edge[:, 0] = spot // columns >= 1
    edge[:, 1] = spot // columns < height - 1
    edge[:, 2] = spot % columns >= 1
    edge[:, 3] = spot % columns < columns - 1

    dims = (n_dp, n_ts, frames, places, columns, team, share, pad, rows, window)
    any_space = pl.BlockSpec(memory_space=pltpu.HBM)
    vmem = pl.BlockSpec(memory_space=pltpu.VMEM)
    buffer = lambda *shape: pltpu.VMEM(shape, BF16)
    wide = lambda *shape: pltpu.VMEM(shape, F32)
    factors, grad = pl.pallas_call(
        functools.partial(whole_kernel, dims),
        out_shape=(
            jax.ShapeDtypeStruct((tokens, 3 * head), BF16),
            jax.ShapeDtypeStruct((rows, triple), F32),
        ),
        in_specs=[any_space] * 14,
        out_specs=(vmem, vmem),
        scratch_shapes=[
            buffer(frames, places, channels), buffer(2, places, channels),
            buffer(*conv_weight.shape), buffer(3 * head, width), wide(1, width), wide(1, width),
            buffer(rows, triple), buffer(rows, triple), buffer(tokens, width),
            buffer(team * pad, tokens), buffer(tokens, tokens), buffer(team * pad, team * pad),
            buffer(tokens, 128),
            buffer(REDUCERS, 24, 128), buffer(REDUCERS, 48, 128), buffer(REDUCERS, 24, 128),
            buffer(n, 24, 128), buffer(n, 48, 128), buffer(n, 24, 128),
            buffer(REDUCERS, 24, 128), buffer(REDUCERS, 48, 128), buffer(REDUCERS, 24, 128),
            buffer(team, pad, triple), buffer(team, pad, triple),
            buffer(team, pad, head), buffer(team, pad, head),
            buffer(team, pad, triple), buffer(team, pad, triple),
            buffer(team, pad, head), buffer(team, pad, head),
            wide(2 * head, 2 * head), wide(tokens, 2 * head),
            pltpu.SemaphoreType.DMA((14,)), pltpu.SemaphoreType.DMA((11,)),
            pltpu.SemaphoreType.DMA((11,)),
        ],
        compiler_params=pltpu.CompilerParams(
            collective_id=0, has_side_effects=True, vmem_limit_bytes=56 * 1024 * 1024
        ),
    )(
        clip_video.reshape(frames, places, channels),
        conv_weight,
        embed_weight,
        gain_spatial.reshape(1, width),
        gain_temporal.reshape(1, width),
        input_spatial,
        input_temporal,
        output_spatial,
        output_temporal,
        cotangent.reshape(tokens, width),
        jnp.asarray(perm, BF16),
        jnp.asarray(frame_bias, BF16),
        jnp.asarray(clip_bias, BF16),
        jnp.asarray(edge, BF16),
    )
    chunk = width // 5
    column = lambda i: (0, i)
    fixed = lambda i: (0, 0)
    output, grad = pl.pallas_call(
        final_kernel,
        grid=(5,),
        out_shape=(
            jax.ShapeDtypeStruct((tokens, width), BF16),
            jax.ShapeDtypeStruct((rows, triple), F32),
        ),
        in_specs=[
            pl.BlockSpec((tokens, 3 * head), fixed),
            pl.BlockSpec((rows, triple), fixed),
            pl.BlockSpec((head, chunk), column),
            pl.BlockSpec((head, chunk), column),
            pl.BlockSpec((head, chunk), column),
        ],
        out_specs=(pl.BlockSpec((tokens, chunk), column), pl.BlockSpec((rows, triple), fixed)),
    )(factors, grad, embed_weight, output_spatial, output_temporal)
    return output.reshape(frames, height, columns, width), grad


def solution(mesh):
    placed = (
        P(("dp", "ts"), None, None, None), P(), P(), P(), P(), P(("dp", "ts"), None),
        P(("dp", "ts"), None), P(), P(), P(("dp", "ts"), None, None, None),
    )
    return jax.shard_map(
        shards,
        mesh=mesh,
        in_specs=placed,
        out_specs=(P(("dp", "ts"), None, None, None), P(("dp", "ts"), None)),
        check_vma=False,
    )
```

```python
import functools

import jax
import jax.numpy as jnp
import numpy as np
from jax import lax
from jax.experimental import pallas as pl
from jax.experimental.pallas import tpu as pltpu
from jax.sharding import PartitionSpec as P

FR = 16
REDUCERS = 16
epsilon = 1e-06
masked = -1e30
F32 = jnp.float32
BF16 = jnp.bfloat16
MESH = pl.DeviceIdType.MESH


def mm(a, b, dims=((1,), (0,))):
    return lax.dot_general(a, b, (dims, ((), ())), preferred_element_type=F32)


def mm_t(a, b):
    return mm(a, b, ((1,), (1,)))


def t_mm(a, b):
    return mm(a, b, ((0,), (0,)))


def wide_mm(a, b):
    high = b.astype(BF16)
    low = (b - high.astype(F32)).astype(BF16)
    return mm(a, high) + mm(a, low)


def attend_forward(q, k, v, bias):
    scores = mm_t(q, k) * q.shape[-1] ** -0.5 + bias.astype(F32)
    raised = jnp.exp(scores - jnp.max(scores, axis=-1, keepdims=True))
    attend = raised / jnp.sum(raised, axis=-1, keepdims=True)
    return mm(attend.astype(BF16), v).astype(BF16), attend


def attend_backward(q, k, v, attend, g):
    scale = q.shape[-1] ** -0.5
    grad_attend = mm_t(g, v)
    grad_values = t_mm(attend.astype(BF16), g)
    inner = jnp.sum(grad_attend * attend, axis=-1, keepdims=True)
    grad_scores = (attend * (grad_attend - inner)).astype(BF16)
    grad_q = mm(grad_scores, k) * scale
    grad_k = t_mm(grad_scores, q) * scale
    return jnp.concatenate([grad_q, grad_k, grad_values], axis=-1).astype(BF16)


def stacked(block):
    third = block.shape[1] // 3
    return jnp.concatenate([block[:, i * third : (i + 1) * third] for i in range(3)], axis=0)


def unstacked(block):
    third = block.shape[0] // 3
    return jnp.concatenate([block[i * third : (i + 1) * third] for i in range(3)], axis=1)


def moved(block, distance):
    if distance == 0:
        return block
    return pltpu.roll(block, distance % block.shape[0], 0)


def whole_kernel(
    dims,
    video_hbm, conv_hbm, embed_hbm, gain_s_hbm, gain_t_hbm, in_s_hbm, in_t_hbm, out_s_hbm,
    out_t_hbm, cot_hbm, perm_hbm, frame_bias_hbm, clip_bias_hbm, edge_hbm,
    result, grad_result,
    video, prior, taps, basis, gain_s, gain_t, in_s, in_t, cot, perm, frame_bias, clip_bias, edge,
    part_a, part_b, part_c, land_a, land_b, land_c, full_a, full_b, full_c,
    sent, got, sent_g, got_g, back, home, back_m, home_m, gram, direct,
    local_sem, send_sem, recv_sem,
):
    n_dp, n_ts, frames, places, columns, team, share, pad, rows, window = dims
    n = n_dp * n_ts
    head = 128
    width = basis.shape[1]
    tokens = frames * places
    dp, ts = lax.axis_index("dp"), lax.axis_index("ts")
    me = dp * n_ts + ts

    loads = [
        (in_s_hbm, in_s), (in_t_hbm, in_t), (gain_s_hbm, gain_s), (gain_t_hbm, gain_t),
        (embed_hbm, basis.at[0:head]), (out_s_hbm, basis.at[head : 2 * head]),
        (video_hbm, video), (edge_hbm, edge), (conv_hbm, taps), (frame_bias_hbm, frame_bias),
        (perm_hbm, perm), (out_t_hbm, basis.at[2 * head : 3 * head]), (cot_hbm, cot),
        (clip_bias_hbm, clip_bias),
    ]
    copies = [pltpu.make_async_copy(s, d, local_sem.at[i]) for i, (s, d) in enumerate(loads)]
    for copy in copies:
        copy.start()

    barrier = pltpu.get_barrier_semaphore()

    def greet(i, carry):
        dev = lax.rem(me + i, n)
        pl.semaphore_signal(
            barrier, inc=1, device_id=(dev // n_ts, lax.rem(dev, n_ts)), device_id_type=MESH
        )
        return carry

    lax.fori_loop(1, n, greet, 0)

    def remote(src, dst, index, dev):
        return pltpu.make_async_remote_copy(
            src_ref=src, dst_ref=dst, send_sem=send_sem.at[index], recv_sem=recv_sem.at[index],
            device_id=(dev // n_ts, lax.rem(dev, n_ts)), device_id_type=MESH,
        )

    def settle(ref, count, sem):
        piece = ref.at[pl.ds(0, count)]
        pltpu.make_async_copy(piece, piece, sem).wait()

    half, quarter = n_ts // 2, n_ts // 4
    mine = dp * half + ts - quarter
    leads = jnp.logical_and(
        jnp.logical_and(ts >= quarter, ts < quarter + half), mine < REDUCERS
    )

    def scatter(part, land, index):
        def step(i, carry):
            r = lax.rem(me + i, REDUCERS)
            dev = r // half * n_ts + quarter + lax.rem(r, half)

            @pl.when(dev != me)
            def _():
                remote(part.at[r], land.at[me], index, dev).start()

            return carry

        lax.fori_loop(0, REDUCERS, step, 0)

    def gather(part, land, full, index):
        @pl.when(leads)
        def _():
            land[pl.ds(me, 1)] = part[pl.ds(mine, 1)]
            settle(land, n - 1, recv_sem.at[index])
            total = jnp.sum(land[...].astype(F32), axis=0, keepdims=True)
            full[pl.ds(mine, 1)] = total.astype(BF16)

            def step(i, carry):
                dev = lax.rem(me + i, n)
                remote(full.at[mine], full.at[mine], index + 1, dev).start()
                return carry

            lax.fori_loop(1, n, step, 0)

    def collect(part, land, full, index):
        @pl.when(leads)
        def _():
            settle(full, REDUCERS - 1, recv_sem.at[index + 1])
            settle(part, REDUCERS - 1, send_sem.at[index])
            settle(land, n - 1, send_sem.at[index + 1])

        @pl.when(jnp.logical_not(leads))
        def _():
            settle(full, REDUCERS, recv_sem.at[index + 1])
            settle(part, REDUCERS, send_sem.at[index])

        return unstacked(full[...].astype(F32).reshape(-1, head)).astype(BF16)

    for copy in copies[:6]:
        copy.wait()
    first = me * rows
    start = pl.multiple_of(first // 128 * 128, 128)
    if (n * rows - rows) // 128 * 128 + window > width:
        limit = width - window
        start = pl.multiple_of(jnp.where(start > limit, limit, start), 128)
    shift = first - start
    place = lax.broadcasted_iota(jnp.int32, (window, rows), 0)
    source = lax.broadcasted_iota(jnp.int32, (window, rows), 1)
    chosen = jnp.where(place == source + shift, 1.0, 0.0).astype(BF16)
    spread_s = mm(chosen, in_s[...]).astype(BF16)
    spread_t = mm(chosen, in_t[...]).astype(BF16)
    span = basis[0 : 2 * head, pl.ds(start, window)].astype(F32)
    span_s = (span[:head] * gain_s[:, pl.ds(start, window)]).astype(BF16)
    span_t = (span * gain_t[:, pl.ds(start, window)]).astype(BF16)
    part_a[...] = stacked(mm(span_s, spread_s)).reshape(part_a.shape).astype(BF16)
    part_b[...] = stacked(mm(span_t, spread_t)).reshape(part_b.shape).astype(BF16)
    copies[6].wait()

    pl.semaphore_wait(barrier, n - 1)
    halo = remote(video.at[pl.ds(frames - 2, 2)], prior, 0, me + 1)
    halo_in = remote(video.at[pl.ds(frames - 2, 2)], prior, 0, me)

    @pl.when(ts < n_ts - 1)
    def _():
        halo.start()

    scatter(part_a, land_a, 1)
    scatter(part_b, land_b, 3)
    embed_rows = mm(span_s, chosen).astype(BF16)

    @pl.when(ts == 0)
    def _():
        prior[...] = jnp.zeros_like(prior)

    @pl.when(ts > 0)
    def _():
        halo_in.wait_recv()

    for copy in copies[7:11]:
        copy.wait()
    volume = jnp.concatenate([prior[...], video[...]], axis=0)
    deep = jnp.concatenate(
        [volume[2 - a : 2 - a + frames].reshape(tokens, head) for a in range(3)], axis=1
    )
    edges = edge[...].astype(F32)
    by_col = [None, None, None]
    for b in range(3):
        weight = jnp.concatenate(
            [jnp.concatenate([taps[a, b, e] for a in range(3)], axis=0) for e in range(3)], axis=1
        )
        product = mm(deep, weight)
        product = moved(product, -(b - 1) * columns)
        if b == 0:
            product = product * edges[:, 0:1]
        if b == 2:
            product = product * edges[:, 1:2]
        for e in range(3):
            piece = product[:, e * head : (e + 1) * head]
            by_col[e] = piece if by_col[e] is None else by_col[e] + piece
    summed = (
        by_col[1] + moved(by_col[0], 1) * edges[:, 2:3] + moved(by_col[2], -1) * edges[:, 3:4]
    )
    features = jax.nn.gelu(summed, approximate=True).astype(BF16)

    gather(part_a, land_a, full_a, 1)

    for copy in copies[11:]:
        copy.wait()
    chunk = width // 5
    gram[...] = jnp.zeros_like(gram)
    direct[...] = jnp.zeros_like(direct)

    def slab(i, carry):
        cols = pl.ds(pl.multiple_of(i * chunk, 128), chunk)
        pair = basis[0 : 2 * head, cols]
        gram[...] += mm_t(pair, pair)
        direct[...] += mm_t(cot[:, cols], basis[head : 3 * head, cols])
        return carry

    lax.fori_loop(0, 5, slab, 0)
    grad_mix_time = direct[:, head:].astype(BF16)
    grams = gram[...]

    seat = lax.rem(ts, team)
    base = me - seat
    order = perm[...]

    def swap(source_ref, target_ref, index):
        def step(i, carry):
            other = lax.rem(seat + i, team)
            remote(source_ref.at[other], target_ref.at[seat], index, base + other).start()
            return carry

        lax.fori_loop(1, team, step, 0)
        target_ref[pl.ds(seat, 1)] = source_ref[pl.ds(seat, 1)]

    def dealt(values, ref):
        ref[...] = mm(order, values).reshape(ref.shape).astype(BF16)

    def received(ref, index):
        settle(ref, team - 1, recv_sem.at[index])
        return ref[...].astype(F32).reshape(team * pad, -1).astype(BF16)

    dealt(grad_mix_time, sent_g)
    swap(sent_g, got_g, 9)
    gather(part_b, land_b, full_b, 3)

    squares = jnp.sum(
        wide_mm(features, grams[:head, :head]) * features.astype(F32), axis=-1, keepdims=True
    )
    factor_one = lax.rsqrt(jnp.maximum(squares, 0.0) / width + epsilon)
    map_space = collect(part_a, land_a, full_a, 1)
    packed_one = (mm(features, map_space) * factor_one).astype(BF16)
    q, k, v = packed_one[:, :head], packed_one[:, head : 2 * head], packed_one[:, 2 * head :]
    mixture_one, attend_one = attend_forward(q, k, v, frame_bias[...])
    joint = jnp.concatenate([features, mixture_one], axis=-1)
    spread = wide_mm(joint, grams)
    squares = jnp.sum(spread * joint.astype(F32), axis=-1, keepdims=True)
    factor_two = lax.rsqrt(jnp.maximum(squares, 0.0) / width + epsilon)
    map_time = collect(part_b, land_b, full_b, 3)
    packed_two = (mm(joint, map_time) * factor_two).astype(BF16)

    dealt(packed_two, sent)
    swap(sent, got, 5)
    tg = received(got_g, 9)
    arrived = received(got, 5)
    tq, tk, tv = (arrived[:, i * head : (i + 1) * head] for i in range(3))
    mixture_two, attend_two = attend_forward(tq, tk, tv, clip_bias[...])
    grad_two = attend_backward(tq, tk, tv, attend_two, tg)
    back[...] = grad_two.astype(F32).reshape(back.shape).astype(BF16)
    swap(back, home, 6)
    back_m[...] = mixture_two.astype(F32).reshape(back_m.shape).astype(BF16)
    swap(back_m, home_m, 10)
    grad_two = t_mm(order, received(home, 6)).astype(BF16)

    inner = jnp.sum(grad_two.astype(F32) * packed_two.astype(F32), axis=-1, keepdims=True)
    grad_mix_one = (
        direct[:, :head]
        + factor_two * mm_t(grad_two, map_time[head:])
        - (factor_two * factor_two * inner / width) * spread[:, head:]
    ).astype(BF16)
    grad_one = attend_backward(q, k, v, attend_one, grad_mix_one)
    scaled = (features.astype(F32) * factor_one).astype(BF16)
    part_c[...] = stacked(t_mm(scaled, grad_one)).reshape(part_c.shape).astype(BF16)
    scatter(part_c, land_c, 7)

    mixture_two = t_mm(order, received(home_m, 10)).astype(BF16)
    triple = jnp.concatenate([joint, mixture_two], axis=-1)

    def write(i, carry):
        cols = pl.ds(pl.multiple_of(i * chunk, 128), chunk)
        result[:, cols] = mm(triple, basis[:, cols]).astype(BF16)
        return carry

    lax.fori_loop(0, 2, write, 0)
    gather(part_c, land_c, full_c, 7)
    lax.fori_loop(2, 5, write, 0)
    total = collect(part_c, land_c, full_c, 7)
    grad_result[...] = t_mm(embed_rows, total)

    @pl.when(ts < n_ts - 1)
    def _():
        halo.wait_send()

    settle(sent, team - 1, send_sem.at[5])
    settle(back, team - 1, send_sem.at[6])
    settle(sent_g, team - 1, send_sem.at[9])
    settle(back_m, team - 1, send_sem.at[10])


def shards(
    clip_video, conv_weight, embed_weight, gain_spatial, gain_temporal, input_spatial,
    input_temporal, output_spatial, output_temporal, cotangent,
):
    frames, height, columns, channels = clip_video.shape
    rows, triple = input_spatial.shape
    head = triple // 3
    width = embed_weight.shape[-1]
    places = height * columns
    tokens = frames * places
    n_dp, n_ts = lax.axis_size("dp"), lax.axis_size("ts")
    n = n_dp * n_ts
    team = FR // frames
    share = places // team
    pad = -(-frames * share // 8) * 8
    reach = max(i * rows % 128 + rows for i in range(n))
    window = -(-reach // 128) * 128

    token = np.arange(tokens)
    frame, spot = token // places, token % places
    slot = spot // share * pad + frame * share + spot % share
    perm = np.zeros((team * pad, tokens), np.float32)
    perm[slot, token] = 1.0
    frame_bias = np.where(frame[:, None] == frame[None, :], 0.0, masked)
    seat = np.arange(team * pad)
    local = seat % pad
    when = seat // pad * frames + local // share
    valid = local < frames * share
    allowed = (
        (local[:, None] % share == local[None, :] % share)
        & (when[:, None] >= when[None, :])
        & valid[:, None]
        & valid[None, :]
    )
    clip_bias = np.where(allowed, 0.0, masked)
    edge = np.zeros((tokens, 128), np.float32)
    edge[:, 0] = spot // columns >= 1
    edge[:, 1] = spot // columns < height - 1
    edge[:, 2] = spot % columns >= 1
    edge[:, 3] = spot % columns < columns - 1

    dims = (n_dp, n_ts, frames, places, columns, team, share, pad, rows, window)
    any_space = pl.BlockSpec(memory_space=pltpu.HBM)
    vmem = pl.BlockSpec(memory_space=pltpu.VMEM)
    buffer = lambda *shape: pltpu.VMEM(shape, BF16)
    wide = lambda *shape: pltpu.VMEM(shape, F32)
    output, grad = pl.pallas_call(
        functools.partial(whole_kernel, dims),
        out_shape=(
            jax.ShapeDtypeStruct((tokens, width), BF16),
            jax.ShapeDtypeStruct((rows, triple), F32),
        ),
        in_specs=[any_space] * 14,
        out_specs=(vmem, vmem),
        scratch_shapes=[
            buffer(frames, places, channels), buffer(2, places, channels),
            buffer(*conv_weight.shape), buffer(3 * head, width), wide(1, width), wide(1, width),
            buffer(rows, triple), buffer(rows, triple), buffer(tokens, width),
            buffer(team * pad, tokens), buffer(tokens, tokens), buffer(team * pad, team * pad),
            buffer(tokens, 128),
            buffer(REDUCERS, 24, 128), buffer(REDUCERS, 48, 128), buffer(REDUCERS, 24, 128),
            buffer(n, 24, 128), buffer(n, 48, 128), buffer(n, 24, 128),
            buffer(REDUCERS, 24, 128), buffer(REDUCERS, 48, 128), buffer(REDUCERS, 24, 128),
            buffer(team, pad, triple), buffer(team, pad, triple),
            buffer(team, pad, head), buffer(team, pad, head),
            buffer(team, pad, triple), buffer(team, pad, triple),
            buffer(team, pad, head), buffer(team, pad, head),
            wide(2 * head, 2 * head), wide(tokens, 2 * head),
            pltpu.SemaphoreType.DMA((14,)), pltpu.SemaphoreType.DMA((11,)),
            pltpu.SemaphoreType.DMA((11,)),
        ],
        compiler_params=pltpu.CompilerParams(
            collective_id=0, has_side_effects=True, vmem_limit_bytes=36 * 1024 * 1024
        ),
    )(*(pltpu.with_memory_space_constraint(x, pltpu.HBM) for x in (
        clip_video.reshape(frames, places, channels),
        conv_weight,
        embed_weight,
        gain_spatial.reshape(1, width),
        gain_temporal.reshape(1, width),
        input_spatial,
        input_temporal,
        output_spatial,
        output_temporal,
        cotangent.reshape(tokens, width),
        jnp.asarray(perm, BF16),
        jnp.asarray(frame_bias, BF16),
        jnp.asarray(clip_bias, BF16),
        jnp.asarray(edge, BF16),
    )))
    return output.reshape(frames, height, columns, width), grad


def solution(mesh):
    placed = (
        P(("dp", "ts"), None, None, None), P(), P(), P(), P(), P(("dp", "ts"), None),
        P(("dp", "ts"), None), P(), P(), P(("dp", "ts"), None, None, None),
    )
    return jax.shard_map(
        shards,
        mesh=mesh,
        in_specs=placed,
        out_specs=(P(("dp", "ts"), None, None, None), P(("dp", "ts"), None)),
        check_vma=False,
    )
```

```python
import functools

import jax
import jax.numpy as jnp
import numpy as np
from jax import lax
from jax.experimental import pallas as pl
from jax.experimental.pallas import tpu as pltpu
from jax.sharding import PartitionSpec as P

FR = 16
REDUCERS = 16
epsilon = 1e-06
masked = -1e30
F32 = jnp.float32
BF16 = jnp.bfloat16
MESH = pl.DeviceIdType.MESH


def mm(a, b, dims=((1,), (0,))):
    return lax.dot_general(a, b, (dims, ((), ())), preferred_element_type=F32)


def mm_t(a, b):
    return mm(a, b, ((1,), (1,)))


def t_mm(a, b):
    return mm(a, b, ((0,), (0,)))


def wide_mm(a, b):
    high = b.astype(BF16)
    low = (b - high.astype(F32)).astype(BF16)
    return mm(a, high) + mm(a, low)


def attend_forward(q, k, v, bias):
    scores = mm_t(q, k) * q.shape[-1] ** -0.5 + bias.astype(F32)
    raised = jnp.exp(scores - jnp.max(scores, axis=-1, keepdims=True))
    attend = raised / jnp.sum(raised, axis=-1, keepdims=True)
    return mm(attend.astype(BF16), v).astype(BF16), attend


def attend_backward(q, k, v, attend, g):
    scale = q.shape[-1] ** -0.5
    grad_attend = mm_t(g, v)
    grad_values = t_mm(attend.astype(BF16), g)
    inner = jnp.sum(grad_attend * attend, axis=-1, keepdims=True)
    grad_scores = (attend * (grad_attend - inner)).astype(BF16)
    grad_q = mm(grad_scores, k) * scale
    grad_k = t_mm(grad_scores, q) * scale
    return jnp.concatenate([grad_q, grad_k, grad_values], axis=-1).astype(BF16)


def stacked(block):
    third = block.shape[1] // 3
    return jnp.concatenate([block[:, i * third : (i + 1) * third] for i in range(3)], axis=0)


def unstacked(block):
    third = block.shape[0] // 3
    return jnp.concatenate([block[i * third : (i + 1) * third] for i in range(3)], axis=1)


def moved(block, distance):
    if distance == 0:
        return block
    return pltpu.roll(block, distance % block.shape[0], 0)


def whole_kernel(
    dims,
    video_hbm, conv_hbm, embed_hbm, gain_s_hbm, gain_t_hbm, in_s_hbm, in_t_hbm, out_s_hbm,
    out_t_hbm, cot_hbm, perm_hbm, frame_bias_hbm, clip_bias_hbm, edge_hbm,
    result, grad_result,
    video, prior, taps, basis, gain_s, gain_t, in_s, in_t, cot, perm, frame_bias, clip_bias, edge,
    twin_a, twin_b, pre_a, pre_b, part_a, part_b, part_c, land_a, land_b, land_c, full_a, full_b, full_c,
    sent, got, sent_g, got_g, back, home, back_m, home_m, gram, direct,
    local_sem, send_sem, recv_sem,
):
    n_dp, n_ts, frames, places, columns, team, share, pad, rows, window = dims
    n = n_dp * n_ts
    head = 128
    width = basis.shape[1]
    tokens = frames * places
    dp, ts = lax.axis_index("dp"), lax.axis_index("ts")
    me = dp * n_ts + ts

    loads = [
        (in_s_hbm, in_s), (in_t_hbm, in_t), (gain_s_hbm, gain_s), (gain_t_hbm, gain_t),
        (embed_hbm, basis.at[0:head]), (out_s_hbm, basis.at[head : 2 * head]),
        (video_hbm, video), (edge_hbm, edge), (conv_hbm, taps), (frame_bias_hbm, frame_bias),
        (perm_hbm, perm), (out_t_hbm, basis.at[2 * head : 3 * head]), (cot_hbm, cot),
        (clip_bias_hbm, clip_bias),
    ]
    copies = [pltpu.make_async_copy(s, d, local_sem.at[i]) for i, (s, d) in enumerate(loads)]
    for copy in copies:
        copy.start()

    barrier = pltpu.get_barrier_semaphore()

    def greet(i, carry):
        dev = lax.rem(me + i, n)
        pl.semaphore_signal(
            barrier, inc=1, device_id=(dev // n_ts, lax.rem(dev, n_ts)), device_id_type=MESH
        )
        return carry

    lax.fori_loop(1, n, greet, 0)

    def remote(src, dst, index, dev):
        return pltpu.make_async_remote_copy(
            src_ref=src, dst_ref=dst, send_sem=send_sem.at[index], recv_sem=recv_sem.at[index],
            device_id=(dev // n_ts, lax.rem(dev, n_ts)), device_id_type=MESH,
        )

    def settle(ref, count, sem):
        piece = ref.at[pl.ds(0, count)]
        pltpu.make_async_copy(piece, piece, sem).wait()

    half, quarter = n_ts // 2, n_ts // 4
    core = lax.rem(ts, 2)
    partner = me + 1 - 2 * core
    pairs = REDUCERS // 2
    seated = dp * (half // 2) + (ts - quarter) // 2
    mine = core * pairs + seated

    def leader(side, i):
        return i // (half // 2) * n_ts + quarter + 2 * lax.rem(i, half // 2) + side

    leads = jnp.logical_and(
        jnp.logical_and(ts >= quarter, ts < quarter + half), seated < pairs
    )

    def scatter(part, land, index):
        def step(i, carry):
            r = lax.rem(me + i, REDUCERS)
            dev = leader(r // pairs, lax.rem(r, pairs))

            @pl.when(dev != me)
            def _():
                remote(part.at[r], land.at[me], index, dev).start()

            return carry

        lax.fori_loop(0, REDUCERS, step, 0)

    def gather(part, land, full, index):
        @pl.when(leads)
        def _():
            land[pl.ds(me, 1)] = part[pl.ds(mine, 1)]
            settle(land, n - 1, recv_sem.at[index])
            total = jnp.sum(land[...].astype(F32), axis=0, keepdims=True)
            full[pl.ds(mine, 1)] = total.astype(BF16)

            def step(i, carry):
                dev = lax.rem(me + i, n)
                remote(full.at[mine], full.at[mine], index + 1, dev).start()
                return carry

            lax.fori_loop(1, n, step, 0)

    def collect(part, land, full, index):
        @pl.when(leads)
        def _():
            settle(full, REDUCERS - 1, recv_sem.at[index + 1])
            settle(part, REDUCERS - 1, send_sem.at[index])
            settle(land, n - 1, send_sem.at[index + 1])

        @pl.when(jnp.logical_not(leads))
        def _():
            settle(full, REDUCERS, recv_sem.at[index + 1])
            settle(part, REDUCERS, send_sem.at[index])

        return unstacked(full[...].astype(F32).reshape(-1, head)).astype(BF16)

    def pair_start(part, twin, index):
        other = pl.ds((1 - core) * pairs, pairs)
        remote(part.at[other], twin, index, partner).start()

    def pair_scatter(part, twin, pre, land, index, pair_index):
        settle(twin, pairs, recv_sem.at[pair_index])
        own = part[pl.ds(core * pairs, pairs)].astype(F32)
        pre[...] = (own + twin[...].astype(F32)).astype(BF16)

        def step(i, carry):
            r = lax.rem(me // 2 + i, pairs)
            dev = leader(core, r)

            @pl.when(dev != me)
            def _():
                remote(pre.at[r], land.at[me // 2], index, dev).start()

            return carry

        lax.fori_loop(0, pairs, step, 0)

    def pair_gather(pre, land, full, index):
        @pl.when(leads)
        def _():
            land[pl.ds(me // 2, 1)] = pre[pl.ds(seated, 1)]
            settle(land, n // 2 - 1, recv_sem.at[index])
            total = jnp.sum(land[...].astype(F32), axis=0, keepdims=True)
            full[pl.ds(mine, 1)] = total.astype(BF16)

            def step(i, carry):
                dev = 2 * lax.rem(me // 2 + i, n // 2) + core
                remote(full.at[mine], full.at[mine], index + 1, dev).start()
                return carry

            lax.fori_loop(1, n // 2, step, 0)

    def pair_collect(pre, twin, land, full, index, pair_index):
        @pl.when(leads)
        def _():
            settle(full, pairs - 1, recv_sem.at[index + 1])
            settle(pre, pairs - 1, send_sem.at[index])
            settle(land, n // 2 - 1, send_sem.at[index + 1])

        @pl.when(jnp.logical_not(leads))
        def _():
            settle(full, pairs, recv_sem.at[index + 1])
            settle(pre, pairs, send_sem.at[index])

        own = pl.ds(core * pairs, pairs)
        remote(full.at[own], full.at[own], pair_index + 2, partner).start()
        settle(full, pairs, recv_sem.at[pair_index + 2])
        settle(twin, pairs, send_sem.at[pair_index])
        settle(full, pairs, send_sem.at[pair_index + 2])
        return unstacked(full[...].astype(F32).reshape(-1, head)).astype(BF16)

    for copy in copies[:6]:
        copy.wait()
    first = me * rows
    start = pl.multiple_of(first // 128 * 128, 128)
    if (n * rows - rows) // 128 * 128 + window > width:
        limit = width - window
        start = pl.multiple_of(jnp.where(start > limit, limit, start), 128)
    shift = first - start
    place = lax.broadcasted_iota(jnp.int32, (window, rows), 0)
    source = lax.broadcasted_iota(jnp.int32, (window, rows), 1)
    chosen = jnp.where(place == source + shift, 1.0, 0.0).astype(BF16)
    spread_s = mm(chosen, in_s[...]).astype(BF16)
    spread_t = mm(chosen, in_t[...]).astype(BF16)
    span = basis[0 : 2 * head, pl.ds(start, window)].astype(F32)
    span_s = (span[:head] * gain_s[:, pl.ds(start, window)]).astype(BF16)
    span_t = (span * gain_t[:, pl.ds(start, window)]).astype(BF16)
    part_a[...] = stacked(mm(span_s, spread_s)).reshape(part_a.shape).astype(BF16)
    part_b[...] = stacked(mm(span_t, spread_t)).reshape(part_b.shape).astype(BF16)
    copies[6].wait()

    pl.semaphore_wait(barrier, n - 1)
    halo = remote(video.at[pl.ds(frames - 2, 2)], prior, 0, me + 1)
    halo_in = remote(video.at[pl.ds(frames - 2, 2)], prior, 0, me)

    @pl.when(ts < n_ts - 1)
    def _():
        halo.start()

    pair_start(part_a, twin_a, 11)
    pair_start(part_b, twin_b, 12)
    pair_scatter(part_a, twin_a, pre_a, land_a, 1, 11)
    pair_scatter(part_b, twin_b, pre_b, land_b, 3, 12)
    embed_rows = mm(span_s, chosen).astype(BF16)

    @pl.when(ts == 0)
    def _():
        prior[...] = jnp.zeros_like(prior)

    @pl.when(ts > 0)
    def _():
        halo_in.wait_recv()

    for copy in copies[7:11]:
        copy.wait()
    volume = jnp.concatenate([prior[...], video[...]], axis=0)
    deep = jnp.concatenate(
        [volume[2 - a : 2 - a + frames].reshape(tokens, head) for a in range(3)], axis=1
    )
    edges = edge[...].astype(F32)
    by_col = [None, None, None]
    for b in range(3):
        weight = jnp.concatenate(
            [jnp.concatenate([taps[a, b, e] for a in range(3)], axis=0) for e in range(3)], axis=1
        )
        product = mm(deep, weight)
        product = moved(product, -(b - 1) * columns)
        if b == 0:
            product = product * edges[:, 0:1]
        if b == 2:
            product = product * edges[:, 1:2]
        for e in range(3):
            piece = product[:, e * head : (e + 1) * head]
            by_col[e] = piece if by_col[e] is None else by_col[e] + piece
    summed = (
        by_col[1] + moved(by_col[0], 1) * edges[:, 2:3] + moved(by_col[2], -1) * edges[:, 3:4]
    )
    features = jax.nn.gelu(summed, approximate=True).astype(BF16)

    pair_gather(pre_a, land_a, full_a, 1)

    for copy in copies[11:]:
        copy.wait()
    chunk = width // 5
    gram[...] = jnp.zeros_like(gram)
    direct[...] = jnp.zeros_like(direct)

    def slab(i, carry):
        cols = pl.ds(pl.multiple_of(i * chunk, 128), chunk)
        pair = basis[0 : 2 * head, cols]
        gram[...] += mm_t(pair, pair)
        direct[...] += mm_t(cot[:, cols], basis[head : 3 * head, cols])
        return carry

    lax.fori_loop(0, 5, slab, 0)
    grad_mix_time = direct[:, head:].astype(BF16)
    grams = gram[...]

    seat = lax.rem(ts, team)
    base = me - seat
    order = perm[...]

    def swap(source_ref, target_ref, index):
        def step(i, carry):
            other = lax.rem(seat + i, team)
            remote(source_ref.at[other], target_ref.at[seat], index, base + other).start()
            return carry

        lax.fori_loop(1, team, step, 0)
        target_ref[pl.ds(seat, 1)] = source_ref[pl.ds(seat, 1)]

    def dealt(values, ref):
        ref[...] = mm(order, values).reshape(ref.shape).astype(BF16)

    def received(ref, index):
        settle(ref, team - 1, recv_sem.at[index])
        return ref[...].astype(F32).reshape(team * pad, -1).astype(BF16)

    dealt(grad_mix_time, sent_g)
    swap(sent_g, got_g, 9)
    pair_gather(pre_b, land_b, full_b, 3)

    squares = jnp.sum(
        wide_mm(features, grams[:head, :head]) * features.astype(F32), axis=-1, keepdims=True
    )
    factor_one = lax.rsqrt(jnp.maximum(squares, 0.0) / width + epsilon)
    map_space = pair_collect(pre_a, twin_a, land_a, full_a, 1, 11)
    packed_one = (mm(features, map_space) * factor_one).astype(BF16)
    q, k, v = packed_one[:, :head], packed_one[:, head : 2 * head], packed_one[:, 2 * head :]
    mixture_one, attend_one = attend_forward(q, k, v, frame_bias[...])
    joint = jnp.concatenate([features, mixture_one], axis=-1)
    spread = wide_mm(joint, grams)
    squares = jnp.sum(spread * joint.astype(F32), axis=-1, keepdims=True)
    factor_two = lax.rsqrt(jnp.maximum(squares, 0.0) / width + epsilon)
    map_time = pair_collect(pre_b, twin_b, land_b, full_b, 3, 12)
    packed_two = (mm(joint, map_time) * factor_two).astype(BF16)

    dealt(packed_two, sent)
    swap(sent, got, 5)
    tg = received(got_g, 9)
    arrived = received(got, 5)
    tq, tk, tv = (arrived[:, i * head : (i + 1) * head] for i in range(3))
    mixture_two, attend_two = attend_forward(tq, tk, tv, clip_bias[...])
    grad_two = attend_backward(tq, tk, tv, attend_two, tg)
    back[...] = grad_two.astype(F32).reshape(back.shape).astype(BF16)
    swap(back, home, 6)
    back_m[...] = mixture_two.astype(F32).reshape(back_m.shape).astype(BF16)
    swap(back_m, home_m, 10)
    grad_two = t_mm(order, received(home, 6)).astype(BF16)

    inner = jnp.sum(grad_two.astype(F32) * packed_two.astype(F32), axis=-1, keepdims=True)
    grad_mix_one = (
        direct[:, :head]
        + factor_two * mm_t(grad_two, map_time[head:])
        - (factor_two * factor_two * inner / width) * spread[:, head:]
    ).astype(BF16)
    grad_one = attend_backward(q, k, v, attend_one, grad_mix_one)
    scaled = (features.astype(F32) * factor_one).astype(BF16)
    part_c[...] = stacked(t_mm(scaled, grad_one)).reshape(part_c.shape).astype(BF16)
    scatter(part_c, land_c, 7)

    mixture_two = t_mm(order, received(home_m, 10)).astype(BF16)
    triple = jnp.concatenate([joint, mixture_two], axis=-1)

    def write(i, carry):
        cols = pl.ds(pl.multiple_of(i * chunk, 128), chunk)
        result[:, cols] = mm(triple, basis[:, cols]).astype(BF16)
        return carry

    lax.fori_loop(0, 2, write, 0)
    gather(part_c, land_c, full_c, 7)
    lax.fori_loop(2, 5, write, 0)
    total = collect(part_c, land_c, full_c, 7)
    grad_result[...] = t_mm(embed_rows, total)

    @pl.when(ts < n_ts - 1)
    def _():
        halo.wait_send()

    settle(sent, team - 1, send_sem.at[5])
    settle(back, team - 1, send_sem.at[6])
    settle(sent_g, team - 1, send_sem.at[9])
    settle(back_m, team - 1, send_sem.at[10])


def shards(
    clip_video, conv_weight, embed_weight, gain_spatial, gain_temporal, input_spatial,
    input_temporal, output_spatial, output_temporal, cotangent,
):
    frames, height, columns, channels = clip_video.shape
    rows, triple = input_spatial.shape
    head = triple // 3
    width = embed_weight.shape[-1]
    places = height * columns
    tokens = frames * places
    n_dp, n_ts = lax.axis_size("dp"), lax.axis_size("ts")
    n = n_dp * n_ts
    team = FR // frames
    share = places // team
    pad = -(-frames * share // 8) * 8
    reach = max(i * rows % 128 + rows for i in range(n))
    window = -(-reach // 128) * 128

    token = np.arange(tokens)
    frame, spot = token // places, token % places
    slot = spot // share * pad + frame * share + spot % share
    perm = np.zeros((team * pad, tokens), np.float32)
    perm[slot, token] = 1.0
    frame_bias = np.where(frame[:, None] == frame[None, :], 0.0, masked)
    seat = np.arange(team * pad)
    local = seat % pad
    when = seat // pad * frames + local // share
    valid = local < frames * share
    allowed = (
        (local[:, None] % share == local[None, :] % share)
        & (when[:, None] >= when[None, :])
        & valid[:, None]
        & valid[None, :]
    )
    clip_bias = np.where(allowed, 0.0, masked)
    edge = np.zeros((tokens, 128), np.float32)
    edge[:, 0] = spot // columns >= 1
    edge[:, 1] = spot // columns < height - 1
    edge[:, 2] = spot % columns >= 1
    edge[:, 3] = spot % columns < columns - 1

    dims = (n_dp, n_ts, frames, places, columns, team, share, pad, rows, window)
    any_space = pl.BlockSpec(memory_space=pltpu.HBM)
    vmem = pl.BlockSpec(memory_space=pltpu.VMEM)
    buffer = lambda *shape: pltpu.VMEM(shape, BF16)
    wide = lambda *shape: pltpu.VMEM(shape, F32)
    output, grad = pl.pallas_call(
        functools.partial(whole_kernel, dims),
        out_shape=(
            jax.ShapeDtypeStruct((tokens, width), BF16),
            jax.ShapeDtypeStruct((rows, triple), F32),
        ),
        in_specs=[any_space] * 14,
        out_specs=(vmem, vmem),
        scratch_shapes=[
            buffer(frames, places, channels), buffer(2, places, channels),
            buffer(*conv_weight.shape), buffer(3 * head, width), wide(1, width), wide(1, width),
            buffer(rows, triple), buffer(rows, triple), buffer(tokens, width),
            buffer(team * pad, tokens), buffer(tokens, tokens), buffer(team * pad, team * pad),
            buffer(tokens, 128),
            buffer(REDUCERS // 2, 24, 128), buffer(REDUCERS // 2, 48, 128),
            buffer(REDUCERS // 2, 24, 128), buffer(REDUCERS // 2, 48, 128),
            buffer(REDUCERS, 24, 128), buffer(REDUCERS, 48, 128), buffer(REDUCERS, 24, 128),
            buffer(n // 2, 24, 128), buffer(n // 2, 48, 128), buffer(n, 24, 128),
            buffer(REDUCERS, 24, 128), buffer(REDUCERS, 48, 128), buffer(REDUCERS, 24, 128),
            buffer(team, pad, triple), buffer(team, pad, triple),
            buffer(team, pad, head), buffer(team, pad, head),
            buffer(team, pad, triple), buffer(team, pad, triple),
            buffer(team, pad, head), buffer(team, pad, head),
            wide(2 * head, 2 * head), wide(tokens, 2 * head),
            pltpu.SemaphoreType.DMA((14,)), pltpu.SemaphoreType.DMA((15,)),
            pltpu.SemaphoreType.DMA((15,)),
        ],
        compiler_params=pltpu.CompilerParams(
            collective_id=0, has_side_effects=True, vmem_limit_bytes=36 * 1024 * 1024
        ),
    )(*(pltpu.with_memory_space_constraint(x, pltpu.HBM) for x in (
        clip_video.reshape(frames, places, channels),
        conv_weight,
        embed_weight,
        gain_spatial.reshape(1, width),
        gain_temporal.reshape(1, width),
        input_spatial,
        input_temporal,
        output_spatial,
        output_temporal,
        cotangent.reshape(tokens, width),
        jnp.asarray(perm, BF16),
        jnp.asarray(frame_bias, BF16),
        jnp.asarray(clip_bias, BF16),
        jnp.asarray(edge, BF16),
    )))
    return output.reshape(frames, height, columns, width), grad


def solution(mesh):
    placed = (
        P(("dp", "ts"), None, None, None), P(), P(), P(), P(), P(("dp", "ts"), None),
        P(("dp", "ts"), None), P(), P(), P(("dp", "ts"), None, None, None),
    )
    return jax.shard_map(
        shards,
        mesh=mesh,
        in_specs=placed,
        out_specs=(P(("dp", "ts"), None, None, None), P(("dp", "ts"), None)),
        check_vma=False,
    )
```

```python
import functools

import jax
import jax.numpy as jnp
import numpy as np
from jax import lax
from jax.experimental import pallas as pl
from jax.experimental.pallas import tpu as pltpu
from jax.sharding import PartitionSpec as P

FR = 16
REDUCERS = 16
epsilon = 1e-06
masked = -1e30
F32 = jnp.float32
BF16 = jnp.bfloat16
MESH = pl.DeviceIdType.MESH


def mm(a, b, dims=((1,), (0,))):
    return lax.dot_general(a, b, (dims, ((), ())), preferred_element_type=F32)


def mm_t(a, b):
    return mm(a, b, ((1,), (1,)))


def t_mm(a, b):
    return mm(a, b, ((0,), (0,)))


def wide_mm(a, b):
    high = b.astype(BF16)
    low = (b - high.astype(F32)).astype(BF16)
    return mm(a, high) + mm(a, low)


def attend_forward(q, k, v, bias):
    scores = mm_t(q, k) * q.shape[-1] ** -0.5 + bias.astype(F32)
    raised = jnp.exp(scores - jnp.max(scores, axis=-1, keepdims=True))
    attend = raised / jnp.sum(raised, axis=-1, keepdims=True)
    return mm(attend.astype(BF16), v).astype(BF16), attend


def attend_backward(q, k, v, attend, g):
    scale = q.shape[-1] ** -0.5
    grad_attend = mm_t(g, v)
    grad_values = t_mm(attend.astype(BF16), g)
    inner = jnp.sum(grad_attend * attend, axis=-1, keepdims=True)
    grad_scores = (attend * (grad_attend - inner)).astype(BF16)
    grad_q = mm(grad_scores, k) * scale
    grad_k = t_mm(grad_scores, q) * scale
    return jnp.concatenate([grad_q, grad_k, grad_values], axis=-1).astype(BF16)


def stacked(block):
    third = block.shape[1] // 3
    return jnp.concatenate([block[:, i * third : (i + 1) * third] for i in range(3)], axis=0)


def unstacked(block):
    third = block.shape[0] // 3
    return jnp.concatenate([block[i * third : (i + 1) * third] for i in range(3)], axis=1)


def moved(block, distance):
    if distance == 0:
        return block
    return pltpu.roll(block, distance % block.shape[0], 0)


def whole_kernel(
    dims,
    video_hbm, conv_hbm, embed_hbm, gain_s_hbm, gain_t_hbm, in_s_hbm, in_t_hbm, out_s_hbm,
    out_t_hbm, cot_hbm, perm_hbm, frame_bias_hbm, clip_bias_hbm, edge_hbm,
    result, grad_result,
    video, prior, taps, basis, gain_s, gain_t, in_s, in_t, cot, perm, frame_bias, clip_bias, edge,
    twin_c, pre_c, twin_a, twin_b, pre_a, pre_b, part_a, part_b, part_c, land_a, land_b, land_c, full_a, full_b, full_c,
    sent, got, sent_g, got_g, back, home, back_m, home_m, gram, direct,
    local_sem, send_sem, recv_sem,
):
    n_dp, n_ts, frames, places, columns, team, share, pad, rows, window = dims
    n = n_dp * n_ts
    head = 128
    width = basis.shape[1]
    tokens = frames * places
    dp, ts = lax.axis_index("dp"), lax.axis_index("ts")
    me = dp * n_ts + ts

    loads = [
        (in_s_hbm, in_s), (in_t_hbm, in_t), (gain_s_hbm, gain_s), (gain_t_hbm, gain_t),
        (embed_hbm, basis.at[0:head]), (out_s_hbm, basis.at[head : 2 * head]),
        (video_hbm, video), (edge_hbm, edge), (conv_hbm, taps), (frame_bias_hbm, frame_bias),
        (perm_hbm, perm), (out_t_hbm, basis.at[2 * head : 3 * head]), (cot_hbm, cot),
        (clip_bias_hbm, clip_bias),
    ]
    copies = [pltpu.make_async_copy(s, d, local_sem.at[i]) for i, (s, d) in enumerate(loads)]
    for copy in copies:
        copy.start()

    barrier = pltpu.get_barrier_semaphore()

    def greet(i, carry):
        dev = lax.rem(me + i, n)
        pl.semaphore_signal(
            barrier, inc=1, device_id=(dev // n_ts, lax.rem(dev, n_ts)), device_id_type=MESH
        )
        return carry

    lax.fori_loop(1, n, greet, 0)

    def remote(src, dst, index, dev):
        return pltpu.make_async_remote_copy(
            src_ref=src, dst_ref=dst, send_sem=send_sem.at[index], recv_sem=recv_sem.at[index],
            device_id=(dev // n_ts, lax.rem(dev, n_ts)), device_id_type=MESH,
        )

    def settle(ref, count, sem):
        piece = ref.at[pl.ds(0, count)]
        pltpu.make_async_copy(piece, piece, sem).wait()

    half, quarter = n_ts // 2, n_ts // 4
    core = lax.rem(ts, 2)
    partner = me + 1 - 2 * core
    pairs = REDUCERS // 2
    seated = dp * (half // 2) + (ts - quarter) // 2
    mine = core * pairs + seated

    def leader(side, i):
        return i // (half // 2) * n_ts + quarter + 2 * lax.rem(i, half // 2) + side

    leads = jnp.logical_and(
        jnp.logical_and(ts >= quarter, ts < quarter + half), seated < pairs
    )

    def scatter(part, land, index):
        def step(i, carry):
            r = lax.rem(me + i, REDUCERS)
            dev = leader(r // pairs, lax.rem(r, pairs))

            @pl.when(dev != me)
            def _():
                remote(part.at[r], land.at[me], index, dev).start()

            return carry

        lax.fori_loop(0, REDUCERS, step, 0)

    def gather(part, land, full, index):
        @pl.when(leads)
        def _():
            land[pl.ds(me, 1)] = part[pl.ds(mine, 1)]
            settle(land, n - 1, recv_sem.at[index])
            total = jnp.sum(land[...].astype(F32), axis=0, keepdims=True)
            full[pl.ds(mine, 1)] = total.astype(BF16)

            def step(i, carry):
                dev = lax.rem(me + i, n)
                remote(full.at[mine], full.at[mine], index + 1, dev).start()
                return carry

            lax.fori_loop(1, n, step, 0)

    def collect(part, land, full, index):
        @pl.when(leads)
        def _():
            settle(full, REDUCERS - 1, recv_sem.at[index + 1])
            settle(part, REDUCERS - 1, send_sem.at[index])
            settle(land, n - 1, send_sem.at[index + 1])

        @pl.when(jnp.logical_not(leads))
        def _():
            settle(full, REDUCERS, recv_sem.at[index + 1])
            settle(part, REDUCERS, send_sem.at[index])

        return unstacked(full[...].astype(F32).reshape(-1, head)).astype(BF16)

    def pair_start(part, twin, index):
        other = pl.ds((1 - core) * pairs, pairs)
        remote(part.at[other], twin, index, partner).start()

    def pair_scatter(part, twin, pre, land, index, pair_index):
        settle(twin, pairs, recv_sem.at[pair_index])
        own = part[pl.ds(core * pairs, pairs)].astype(F32)
        pre[...] = (own + twin[...].astype(F32)).astype(BF16)

        def step(i, carry):
            r = lax.rem(me // 2 + i, pairs)
            dev = leader(core, r)

            @pl.when(dev != me)
            def _():
                remote(pre.at[r], land.at[me // 2], index, dev).start()

            return carry

        lax.fori_loop(0, pairs, step, 0)

    def pair_gather(pre, land, full, index):
        @pl.when(leads)
        def _():
            land[pl.ds(me // 2, 1)] = pre[pl.ds(seated, 1)]
            settle(land, n // 2 - 1, recv_sem.at[index])
            total = jnp.sum(land[...].astype(F32), axis=0, keepdims=True)
            full[pl.ds(mine, 1)] = total.astype(BF16)

            def step(i, carry):
                dev = 2 * lax.rem(me // 2 + i, n // 2) + core
                remote(full.at[mine], full.at[mine], index + 1, dev).start()
                return carry

            lax.fori_loop(1, n // 2, step, 0)

    def pair_collect(pre, twin, land, full, index, pair_index):
        @pl.when(leads)
        def _():
            settle(full, pairs - 1, recv_sem.at[index + 1])
            settle(pre, pairs - 1, send_sem.at[index])
            settle(land, n // 2 - 1, send_sem.at[index + 1])

        @pl.when(jnp.logical_not(leads))
        def _():
            settle(full, pairs, recv_sem.at[index + 1])
            settle(pre, pairs, send_sem.at[index])

        own = pl.ds(core * pairs, pairs)
        remote(full.at[own], full.at[own], pair_index + 2, partner).start()
        settle(full, pairs, recv_sem.at[pair_index + 2])
        settle(twin, pairs, send_sem.at[pair_index])
        settle(full, pairs, send_sem.at[pair_index + 2])
        return unstacked(full[...].astype(F32).reshape(-1, head)).astype(BF16)

    for copy in copies[:6]:
        copy.wait()
    first = me * rows
    start = pl.multiple_of(first // 128 * 128, 128)
    if (n * rows - rows) // 128 * 128 + window > width:
        limit = width - window
        start = pl.multiple_of(jnp.where(start > limit, limit, start), 128)
    shift = first - start
    place = lax.broadcasted_iota(jnp.int32, (window, rows), 0)
    source = lax.broadcasted_iota(jnp.int32, (window, rows), 1)
    chosen = jnp.where(place == source + shift, 1.0, 0.0).astype(BF16)
    spread_s = mm(chosen, in_s[...]).astype(BF16)
    spread_t = mm(chosen, in_t[...]).astype(BF16)
    span = basis[0 : 2 * head, pl.ds(start, window)].astype(F32)
    span_s = (span[:head] * gain_s[:, pl.ds(start, window)]).astype(BF16)
    span_t = (span * gain_t[:, pl.ds(start, window)]).astype(BF16)
    part_a[...] = stacked(mm(span_s, spread_s)).reshape(part_a.shape).astype(BF16)
    part_b[...] = stacked(mm(span_t, spread_t)).reshape(part_b.shape).astype(BF16)
    copies[6].wait()

    pl.semaphore_wait(barrier, n - 1)
    halo = remote(video.at[pl.ds(frames - 2, 2)], prior, 0, me + 1)
    halo_in = remote(video.at[pl.ds(frames - 2, 2)], prior, 0, me)

    @pl.when(ts < n_ts - 1)
    def _():
        halo.start()

    pair_start(part_a, twin_a, 11)
    pair_start(part_b, twin_b, 12)
    pair_scatter(part_a, twin_a, pre_a, land_a, 1, 11)
    pair_scatter(part_b, twin_b, pre_b, land_b, 3, 12)
    embed_rows = mm(span_s, chosen).astype(BF16)

    @pl.when(ts == 0)
    def _():
        prior[...] = jnp.zeros_like(prior)

    @pl.when(ts > 0)
    def _():
        halo_in.wait_recv()

    for copy in copies[7:11]:
        copy.wait()
    volume = jnp.concatenate([prior[...], video[...]], axis=0)
    deep = jnp.concatenate(
        [volume[2 - a : 2 - a + frames].reshape(tokens, head) for a in range(3)], axis=1
    )
    edges = edge[...].astype(F32)
    by_col = [None, None, None]
    for b in range(3):
        weight = jnp.concatenate(
            [jnp.concatenate([taps[a, b, e] for a in range(3)], axis=0) for e in range(3)], axis=1
        )
        product = mm(deep, weight)
        product = moved(product, -(b - 1) * columns)
        if b == 0:
            product = product * edges[:, 0:1]
        if b == 2:
            product = product * edges[:, 1:2]
        for e in range(3):
            piece = product[:, e * head : (e + 1) * head]
            by_col[e] = piece if by_col[e] is None else by_col[e] + piece
    summed = (
        by_col[1] + moved(by_col[0], 1) * edges[:, 2:3] + moved(by_col[2], -1) * edges[:, 3:4]
    )
    features = jax.nn.gelu(summed, approximate=True).astype(BF16)

    pair_gather(pre_a, land_a, full_a, 1)

    for copy in copies[11:]:
        copy.wait()
    chunk = width // 5
    gram[...] = jnp.zeros_like(gram)
    direct[...] = jnp.zeros_like(direct)

    def slab(i, carry):
        cols = pl.ds(pl.multiple_of(i * chunk, 128), chunk)
        pair = basis[0 : 2 * head, cols]
        gram[...] += mm_t(pair, pair)
        direct[...] += mm_t(cot[:, cols], basis[head : 3 * head, cols])
        return carry

    lax.fori_loop(0, 5, slab, 0)
    grad_mix_time = direct[:, head:].astype(BF16)
    grams = gram[...]

    seat = lax.rem(ts, team)
    base = me - seat
    order = perm[...]

    def swap(source_ref, target_ref, index):
        def step(i, carry):
            other = lax.rem(seat + i, team)
            remote(source_ref.at[other], target_ref.at[seat], index, base + other).start()
            return carry

        lax.fori_loop(1, team, step, 0)
        target_ref[pl.ds(seat, 1)] = source_ref[pl.ds(seat, 1)]

    def dealt(values, ref):
        ref[...] = mm(order, values).reshape(ref.shape).astype(BF16)

    def received(ref, index):
        settle(ref, team - 1, recv_sem.at[index])
        return ref[...].astype(F32).reshape(team * pad, -1).astype(BF16)

    dealt(grad_mix_time, sent_g)
    swap(sent_g, got_g, 9)
    pair_gather(pre_b, land_b, full_b, 3)

    squares = jnp.sum(
        wide_mm(features, grams[:head, :head]) * features.astype(F32), axis=-1, keepdims=True
    )
    factor_one = lax.rsqrt(jnp.maximum(squares, 0.0) / width + epsilon)
    map_space = pair_collect(pre_a, twin_a, land_a, full_a, 1, 11)
    packed_one = (mm(features, map_space) * factor_one).astype(BF16)
    q, k, v = packed_one[:, :head], packed_one[:, head : 2 * head], packed_one[:, 2 * head :]
    mixture_one, attend_one = attend_forward(q, k, v, frame_bias[...])
    joint = jnp.concatenate([features, mixture_one], axis=-1)
    spread = wide_mm(joint, grams)
    squares = jnp.sum(spread * joint.astype(F32), axis=-1, keepdims=True)
    factor_two = lax.rsqrt(jnp.maximum(squares, 0.0) / width + epsilon)
    map_time = pair_collect(pre_b, twin_b, land_b, full_b, 3, 12)
    packed_two = (mm(joint, map_time) * factor_two).astype(BF16)

    dealt(packed_two, sent)
    swap(sent, got, 5)
    tg = received(got_g, 9)
    arrived = received(got, 5)
    tq, tk, tv = (arrived[:, i * head : (i + 1) * head] for i in range(3))
    mixture_two, attend_two = attend_forward(tq, tk, tv, clip_bias[...])
    grad_two = attend_backward(tq, tk, tv, attend_two, tg)
    back[...] = grad_two.astype(F32).reshape(back.shape).astype(BF16)
    swap(back, home, 6)
    back_m[...] = mixture_two.astype(F32).reshape(back_m.shape).astype(BF16)
    swap(back_m, home_m, 10)
    grad_two = t_mm(order, received(home, 6)).astype(BF16)

    inner = jnp.sum(grad_two.astype(F32) * packed_two.astype(F32), axis=-1, keepdims=True)
    grad_mix_one = (
        direct[:, :head]
        + factor_two * mm_t(grad_two, map_time[head:])
        - (factor_two * factor_two * inner / width) * spread[:, head:]
    ).astype(BF16)
    grad_one = attend_backward(q, k, v, attend_one, grad_mix_one)
    scaled = (features.astype(F32) * factor_one).astype(BF16)
    part_c[...] = stacked(t_mm(scaled, grad_one)).reshape(part_c.shape).astype(BF16)
    pair_start(part_c, twin_c, 15)
    pair_scatter(part_c, twin_c, pre_c, land_c, 7, 15)

    mixture_two = t_mm(order, received(home_m, 10)).astype(BF16)
    triple = jnp.concatenate([joint, mixture_two], axis=-1)

    def write(i, carry):
        cols = pl.ds(pl.multiple_of(i * chunk, 128), chunk)
        result[:, cols] = mm(triple, basis[:, cols]).astype(BF16)
        return carry

    lax.fori_loop(0, 2, write, 0)
    pair_gather(pre_c, land_c, full_c, 7)
    lax.fori_loop(2, 5, write, 0)
    total = pair_collect(pre_c, twin_c, land_c, full_c, 7, 15)
    grad_result[...] = t_mm(embed_rows, total)

    @pl.when(ts < n_ts - 1)
    def _():
        halo.wait_send()

    settle(sent, team - 1, send_sem.at[5])
    settle(back, team - 1, send_sem.at[6])
    settle(sent_g, team - 1, send_sem.at[9])
    settle(back_m, team - 1, send_sem.at[10])


def shards(
    clip_video, conv_weight, embed_weight, gain_spatial, gain_temporal, input_spatial,
    input_temporal, output_spatial, output_temporal, cotangent,
):
    frames, height, columns, channels = clip_video.shape
    rows, triple = input_spatial.shape
    head = triple // 3
    width = embed_weight.shape[-1]
    places = height * columns
    tokens = frames * places
    n_dp, n_ts = lax.axis_size("dp"), lax.axis_size("ts")
    n = n_dp * n_ts
    team = FR // frames
    share = places // team
    pad = -(-frames * share // 8) * 8
    reach = max(i * rows % 128 + rows for i in range(n))
    window = -(-reach // 128) * 128

    token = np.arange(tokens)
    frame, spot = token // places, token % places
    slot = spot // share * pad + frame * share + spot % share
    perm = np.zeros((team * pad, tokens), np.float32)
    perm[slot, token] = 1.0
    frame_bias = np.where(frame[:, None] == frame[None, :], 0.0, masked)
    seat = np.arange(team * pad)
    local = seat % pad
    when = seat // pad * frames + local // share
    valid = local < frames * share
    allowed = (
        (local[:, None] % share == local[None, :] % share)
        & (when[:, None] >= when[None, :])
        & valid[:, None]
        & valid[None, :]
    )
    clip_bias = np.where(allowed, 0.0, masked)
    edge = np.zeros((tokens, 128), np.float32)
    edge[:, 0] = spot // columns >= 1
    edge[:, 1] = spot // columns < height - 1
    edge[:, 2] = spot % columns >= 1
    edge[:, 3] = spot % columns < columns - 1

    dims = (n_dp, n_ts, frames, places, columns, team, share, pad, rows, window)
    any_space = pl.BlockSpec(memory_space=pltpu.HBM)
    vmem = pl.BlockSpec(memory_space=pltpu.VMEM)
    buffer = lambda *shape: pltpu.VMEM(shape, BF16)
    wide = lambda *shape: pltpu.VMEM(shape, F32)
    output, grad = pl.pallas_call(
        functools.partial(whole_kernel, dims),
        out_shape=(
            jax.ShapeDtypeStruct((tokens, width), BF16),
            jax.ShapeDtypeStruct((rows, triple), F32),
        ),
        in_specs=[any_space] * 14,
        out_specs=(vmem, vmem),
        scratch_shapes=[
            buffer(frames, places, channels), buffer(2, places, channels),
            buffer(*conv_weight.shape), buffer(3 * head, width), wide(1, width), wide(1, width),
            buffer(rows, triple), buffer(rows, triple), buffer(tokens, width),
            buffer(team * pad, tokens), buffer(tokens, tokens), buffer(team * pad, team * pad),
            buffer(tokens, 128),
            buffer(REDUCERS // 2, 24, 128), buffer(REDUCERS // 2, 24, 128),
            buffer(REDUCERS // 2, 24, 128), buffer(REDUCERS // 2, 48, 128),
            buffer(REDUCERS // 2, 24, 128), buffer(REDUCERS // 2, 48, 128),
            buffer(REDUCERS, 24, 128), buffer(REDUCERS, 48, 128), buffer(REDUCERS, 24, 128),
            buffer(n // 2, 24, 128), buffer(n // 2, 48, 128), buffer(n // 2, 24, 128),
            buffer(REDUCERS, 24, 128), buffer(REDUCERS, 48, 128), buffer(REDUCERS, 24, 128),
            buffer(team, pad, triple), buffer(team, pad, triple),
            buffer(team, pad, head), buffer(team, pad, head),
            buffer(team, pad, triple), buffer(team, pad, triple),
            buffer(team, pad, head), buffer(team, pad, head),
            wide(2 * head, 2 * head), wide(tokens, 2 * head),
            pltpu.SemaphoreType.DMA((14,)), pltpu.SemaphoreType.DMA((18,)),
            pltpu.SemaphoreType.DMA((18,)),
        ],
        compiler_params=pltpu.CompilerParams(
            collective_id=0, has_side_effects=True, vmem_limit_bytes=36 * 1024 * 1024
        ),
    )(*(pltpu.with_memory_space_constraint(x, pltpu.HBM) for x in (
        clip_video.reshape(frames, places, channels),
        conv_weight,
        embed_weight,
        gain_spatial.reshape(1, width),
        gain_temporal.reshape(1, width),
        input_spatial,
        input_temporal,
        output_spatial,
        output_temporal,
        cotangent.reshape(tokens, width),
        jnp.asarray(perm, BF16),
        jnp.asarray(frame_bias, BF16),
        jnp.asarray(clip_bias, BF16),
        jnp.asarray(edge, BF16),
    )))
    return output.reshape(frames, height, columns, width), grad


def solution(mesh):
    placed = (
        P(("dp", "ts"), None, None, None), P(), P(), P(), P(), P(("dp", "ts"), None),
        P(("dp", "ts"), None), P(), P(), P(("dp", "ts"), None, None, None),
    )
    return jax.shard_map(
        shards,
        mesh=mesh,
        in_specs=placed,
        out_specs=(P(("dp", "ts"), None, None, None), P(("dp", "ts"), None)),
        check_vma=False,
    )
```
